128 devices in a mesh: row: 8 (over x, core), mp: 16 (over y, z).
Axes of the slice: x: 4, y: 4, z: 4, core: 2. Of those that a mesh axis runs over, the one named last changes fastest.
Arguments:
- queries: bfloat16 [2560, 16384], P('row', 'mp'), may hold values from -16 to 16
- new_kv: bfloat16 [2560, 2048], P('row', 'mp'), may hold values from -9 to 9
- cache_keys: bfloat16 [512, 16, 512, 128], P('row', 'mp'), may hold values from -26 to 26
- cache_values: bfloat16 [512, 16, 512, 128], P('row', 'mp'), may hold values from -12 to 12
- cache_lens: int32 [512], P('row'), may hold values from 8 to 1019, as said below
- accepted: int32 [512], P('row'), may hold values from 0 to 5
- dest: int32 [512], P('row'), may hold values from 0 to 511, as said below
- out_weight: bfloat16 [16384, 16384], P('mp', 'row'), may hold values from -0.046875 to 0.046875
Outputs:
- mixed: bfloat16 [2560, 16384], P('mp', 'row')
- next_kv: bfloat16 [512, 5, 2048], P('row', None, 'mp')
The draws below stay inside these ranges and needn't reach their ends.
Inputs may be any that keep to these rules, and one draw needn't show every extreme that they name: `cache_lens`: every beam's cache leaves room for its 5 new tokens. dest is a permutation of 0 to 511; of the beams in each aligned block of 64 beams, exactly 8 go to slots of each aligned block of 64 slots.
All inputs are finite; a program needn't handle non-finite values.
Results may differ from the reference program's by a relative error of at most 0.02.
Values may be sent and summed in bfloat16 or wider, within the bound.
A program may use at most 128 MiB of HBM per device.

```python
import jax
import jax.numpy as jnp
from jax import lax

D = 16384
HQ = 128
KVH = 8
HD = 128
GROUP = 16
DRAFT = 5
CACHE = 1024
HALF = 512
BEAMS_ROW = 64
BEAMS = 512
TOKENS = 2560
SHARE = 8


def draw_queries(key, part):
    main_key = jax.random.fold_in(key, 3)
    shape = (BEAMS, DRAFT, KVH, HQ // KVH, HD)
    values = jnp.clip(jax.random.normal(main_key, shape, jnp.float32), -6.0, 6.0)
    return values.reshape(TOKENS, HQ * HD).astype(jnp.bfloat16)


def draw_cache_keys(key, part):
    main_key = jax.random.fold_in(key, 5)
    shape = (BEAMS, KVH, 2, HALF, HD)
    values = 1.5 * jnp.clip(jax.random.normal(main_key, shape, jnp.float32), -6.0, 6.0)
    return values.reshape(BEAMS, 2 * KVH, HALF, HD).astype(jnp.bfloat16)


def draw_cache_lens(key, part):
    base_key = jax.random.fold_in(key, 7)
    key_one, key_two, key_three = jax.random.split(base_key, 3)
    top_bits = CACHE.bit_length()
    powers = jax.random.randint(key_one, (BEAMS,), 3, top_bits)
    lower = jnp.left_shift(jnp.int32(1), powers.astype(jnp.int32))
    lengths = jax.random.randint(key_two, (BEAMS,), lower, 2 * lower)
    lengths = jnp.minimum(lengths, CACHE - DRAFT).astype(jnp.int32)
    picked = jax.random.randint(key_three, (), 0, BEAMS)
    lengths = lengths.at[picked].set(CACHE - DRAFT)
    lengths = lengths.at[(picked + 1) % BEAMS].set(8)
    return lengths.astype(jnp.int32)


def draw_dest(key, part):
    base_key = jax.random.fold_in(key, 9)
    key_one, key_two = jax.random.split(base_key)
    blocks = BEAMS_ROW // SHARE
    send_keys = jax.random.split(key_one, blocks)
    land_keys = jax.random.split(key_two, blocks)
    send_order = jax.vmap(lambda k: jax.random.permutation(k, BEAMS_ROW))(send_keys)
    land_order = jax.vmap(lambda k: jax.random.permutation(k, BEAMS_ROW))(land_keys)
    ranks = jnp.argsort(send_order, axis=1).astype(jnp.int32)
    target = ranks // SHARE
    within = ranks % SHARE
    source = jnp.arange(blocks, dtype=jnp.int32)[:, None]
    landing = land_order[target, source * SHARE + within]
    slots = target * BEAMS_ROW + landing
    return slots.reshape(BEAMS).astype(jnp.int32)


def set_ends(values, own_key, smallest, largest):
    index_at = [jax.random.randint(jax.random.fold_in(own_key, axis), (), 0, length) for axis, length in enumerate(values.shape)]
    longest = values.shape.index(max(values.shape))
    neighbour = index_at[:longest] + [(index_at[longest] + 1) % values.shape[longest]] + index_at[longest + 1:]
    return values.at[tuple(index_at)].set(smallest).at[tuple(neighbour)].set(largest)


def block_levels(rng, extent, pieces, least, largest):
    factor_of, own = 1.0, jax.random.fold_in(rng, 6)
    for axis_at, blocks in pieces:
        steps = jnp.exp(jax.random.uniform(jax.random.fold_in(own, axis_at), (blocks,), jnp.float32, least / len(pieces), largest / len(pieces)))
        factor_of = factor_of * jnp.repeat(steps, extent[axis_at] // blocks).reshape([-1 if axis == axis_at else 1 for axis in range(len(extent))])
    return factor_of


def gaussian(own_key, shape, scale, most, cuts=(), kind=jnp.bfloat16):
    array = scale * jax.random.normal(own_key, shape, jnp.float32)
    if cuts:
        array = array * block_levels(own_key, shape, cuts, -0.22, 0.18)
    return jnp.clip(array, -most, most).astype(kind)


def setup_inputs(seed: int = 0) -> dict:
    seeds = jax.random.split(jax.random.key(seed), 9)
    queries = draw_queries(jax.random.fold_in(seeds[8], 71), 0)
    new_kv = gaussian(seeds[1], (TOKENS, 2 * KVH * HD), 1.5, 9.0, ((0, 8), (1, 16)))
    cache_keys = draw_cache_keys(jax.random.fold_in(seeds[8], 71), 0)
    cache_values = gaussian(seeds[3], (BEAMS, 2 * KVH, HALF, HD), 2.0, 12.0, ((0, 8), (1, 16)))
    cache_lens = draw_cache_lens(jax.random.fold_in(seeds[8], 71), 0)
    accepted = set_ends(jax.random.randint(seeds[5], (BEAMS,), 0, DRAFT + 1), jax.random.fold_in(seeds[5], 1), 0, DRAFT).astype(jnp.int32)
    dest = draw_dest(jax.random.fold_in(seeds[8], 71), 0)
    out_weight = gaussian(seeds[7], (HQ * HD, D), (HQ * HD) ** -0.5, 0.046875, ((0, 16), (1, 8)))
    return {"queries": queries, "new_kv": new_kv, "cache_keys": cache_keys, "cache_values": cache_values, "cache_lens": cache_lens, "accepted": accepted, "dest": dest, "out_weight": out_weight}


masked_score = -1e30


def beam_attention(inputs):
    beam_queries, beam_fresh, beam_keys, beam_values, length = inputs
    scale = HD ** -0.5
    query_block = beam_queries.astype(jnp.float32).reshape(DRAFT, KVH, GROUP, HD).transpose(1, 0, 2, 3)
    key_block = beam_keys.astype(jnp.float32).reshape(KVH, 2, HALF, HD)
    value_block = beam_values.astype(jnp.float32).reshape(KVH, 2, HALF, HD)
    fresh_block = beam_fresh.astype(jnp.float32).reshape(DRAFT, KVH, 2, HD).transpose(1, 0, 2, 3)
    fresh_keys = fresh_block[:, :, 0]
    fresh_values = fresh_block[:, :, 1]
    cache_scores = jnp.einsum("gtjd,gsid->gstji", query_block, key_block) * scale
    fresh_scores = jnp.einsum("gtjd,gud->gtju", query_block, fresh_keys) * scale
    halves = jnp.arange(2, dtype=jnp.int32)
    spots = halves[:, None] * HALF + jnp.arange(HALF, dtype=jnp.int32)[None, :]
    cache_valid = spots < length
    order = jnp.arange(DRAFT, dtype=jnp.int32)
    fresh_side = (length + order) // HALF
    fresh_valid = (order[None, :, None] >= order[None, None, :]) & (fresh_side[None, None, :] == halves[:, None, None])
    scores = jnp.concatenate([cache_scores, jnp.broadcast_to(fresh_scores[:, None], (KVH, 2, DRAFT, GROUP, DRAFT))], axis=-1)
    valid = jnp.concatenate([jnp.broadcast_to(cache_valid[None, :, None, None, :], (KVH, 2, DRAFT, GROUP, HALF)), jnp.broadcast_to(fresh_valid[None, :, :, None, :], (KVH, 2, DRAFT, GROUP, DRAFT))], axis=-1)
    masked = jnp.where(valid, scores, masked_score)
    highest = jnp.max(masked, axis=-1)
    weights = jnp.where(valid, jnp.exp(masked - highest[..., None]), 0.0).astype(jnp.bfloat16)
    weights_wide = weights.astype(jnp.float32)
    values_all = jnp.concatenate([value_block, jnp.broadcast_to(fresh_values[:, None], (KVH, 2, DRAFT, HD))], axis=2)
    partial_value = jnp.einsum("gstju,gsud->gstjd", weights_wide, values_all)
    weight_mass = jnp.sum(weights_wide, axis=-1)
    summit = jnp.max(highest, axis=1)
    factor = jnp.exp(highest - summit[:, None])
    numer = jnp.sum(factor[..., None] * partial_value, axis=1)
    denom = jnp.sum(factor * weight_mass, axis=1)
    attention = (numer / denom[..., None]).astype(jnp.bfloat16)
    return attention.transpose(1, 0, 2, 3).reshape(DRAFT, HQ * HD)


def reference(queries, new_kv, cache_keys, cache_values, cache_lens, accepted, dest, out_weight):
    beam_queries = queries.reshape(BEAMS, DRAFT, HQ * HD)
    beam_fresh = new_kv.reshape(BEAMS, DRAFT, 2 * KVH * HD)
    attention = lax.map(beam_attention, (beam_queries, beam_fresh, cache_keys, cache_values, cache_lens))
    attention = attention.reshape(TOKENS, HQ * HD)
    mixed = jnp.dot(attention, out_weight, preferred_element_type=jnp.float32).astype(jnp.bfloat16)
    order = jnp.arange(DRAFT, dtype=jnp.int32)
    kept_mask = order[None, :] < accepted[:, None]
    kept_rows = jnp.where(kept_mask[..., None], beam_fresh, jnp.zeros_like(beam_fresh))
    next_kv = jnp.zeros_like(beam_fresh).at[dest].set(kept_rows)
    return mixed, next_kv
```

```python
import functools

import jax
import jax.numpy as jnp
from jax import lax
from jax.experimental import pallas as pl
from jax.experimental.pallas import tpu as pltpu
from jax.sharding import PartitionSpec as P

MESH = pl.DeviceIdType.MESH
masked_score = -1e30

TREES = ((0, 2, 1, 3), (2, 1, 3, 0), (1, 3, 0, 2), (3, 0, 2, 1))
STEP_BASE = (0, 8, 12, 14)
LAG = 2


def bits_of(place):
    y, z = place // 4, place % 4
    return (((y + 1) // 2) % 2, y // 2, ((z + 1) // 2) % 2, z // 2)


def along(place, direction):
    y, z = place // 4, place % 4
    if direction == 0:
        y = y + 1 - 2 * (y % 2)
    elif direction == 1:
        y = 3 - y
    elif direction == 2:
        z = z + 1 - 2 * (z % 2)
    else:
        z = 3 - z
    return y * 4 + z


def all_of(terms):
    result = terms[0]
    for term in terms[1:]:
        result = jnp.logical_and(result, term)
    return result


def project_kernel(
    attention, weight, fresh, keyed, mixed, next_kv,
    gathered, weight_here, held, inbox, parcels, arrived,
    local_sem, own_send, far_send, gather_recv, tree_send, tree_recv, parcel_send, parcel_recv,
):
    row, mp = lax.axis_index("row"), lax.axis_index("mp")
    x, core = row // 2, row % 2
    sibling = {"row": x * 2 + 1 - core, "mp": mp}
    right = {"row": ((x + 1) % 4) * 2 + core, "mp": mp}
    left = {"row": ((x + 3) % 4) * 2 + core, "mp": mp}
    weight_copy = pltpu.make_async_copy(weight, weight_here, local_sem.at[0])
    weight_copy.start()
    own_copy = pltpu.make_async_copy(attention, gathered.at[0], local_sem.at[1])
    own_copy.start()

    barrier = pltpu.get_barrier_semaphore()
    for step in range(1, 8):
        pl.semaphore_signal(
            barrier, inc=1, device_id={"row": (row + step) % 8, "mp": mp}, device_id_type=MESH
        )
    for direction in range(4):
        pl.semaphore_signal(
            barrier, inc=1, device_id={"row": row, "mp": along(mp, direction)}, device_id_type=MESH
        )
    pl.semaphore_wait(barrier, 11)

    def remote(source, target, send_sem, recv_sem, device):
        return pltpu.make_async_remote_copy(
            src_ref=source, dst_ref=target, send_sem=send_sem, recv_sem=recv_sem,
            device_id=device, device_id_type=MESH,
        )

    half = gathered.shape[1] // 2
    own_copy.wait()
    to_right = remote(gathered.at[0], gathered.at[3], own_send.at[0], gather_recv.at[3], right)
    to_left = remote(gathered.at[0], gathered.at[2], own_send.at[1], gather_recv.at[2], left)
    to_sibling = remote(gathered.at[0], gathered.at[1], own_send.at[2], gather_recv.at[1], sibling)
    to_left.start()
    to_right.start()
    to_sibling.start()
    pass_left = remote(
        gathered.at[2, pl.ds(0, half)], gathered.at[6, pl.ds(0, half)], far_send.at[0], gather_recv.at[6], left
    )
    pass_right = remote(
        gathered.at[3, pl.ds(half, half)], gathered.at[6, pl.ds(half, half)], far_send.at[1], gather_recv.at[8], right
    )
    share_right = remote(gathered.at[2], gathered.at[4], far_send.at[2], gather_recv.at[4], sibling)
    share_left = remote(gathered.at[3], gathered.at[5], far_send.at[3], gather_recv.at[5], sibling)
    share_far = remote(gathered.at[6], gathered.at[7], far_send.at[4], gather_recv.at[7], sibling)

    place = lax.broadcasted_iota(jnp.int32, (64, 320), 0)
    fresh_rows = fresh[...]
    columns = []
    for draft in range(5):
        pick = (keyed[draft : draft + 1, :] == place).astype(jnp.bfloat16)
        columns.append(
            jnp.dot(pick, fresh_rows, preferred_element_type=jnp.float32).astype(jnp.bfloat16)
        )
    label = jnp.sum(
        jnp.where(keyed[5:6, :] == place, keyed[6:7, :], 0).astype(jnp.float32), 1, keepdims=True
    )
    columns.append(jnp.broadcast_to(label, (64, 128)).astype(jnp.bfloat16))
    for block in range(8):
        for part, column in enumerate(columns):
            parcels[block, :, pl.ds(part * 128, 128)] = column[block * 8 : block * 8 + 8]
    own_parcel = pltpu.make_async_copy(parcels.at[row], arrived.at[row], local_sem.at[2])
    own_parcel.start()
    for step in range(1, 8):
        target = (row + step) % 8
        remote(
            parcels.at[target], arrived.at[row], parcel_send.at[step], parcel_recv.at[row],
            {"row": target, "mp": mp},
        ).start()
    weight_copy.wait()

    rows_owned = mixed.shape[0]
    width = held.shape[3]
    my_bits = bits_of(mp)

    def tree_message(tree, step, block):
        order = TREES[tree]
        rest = bits_of(block)
        index = STEP_BASE[step]
        for power, direction in enumerate(order[step + 1 :]):
            index = index + rest[direction] * (1 << power)
        return remote(
            held.at[tree, block], inbox.at[tree, index], tree_send.at[tree, block],
            tree_recv.at[tree, index], {"row": row, "mp": along(mp, order[step])},
        ), index

    def first_block(slot):
        shift = jnp.where(slot < 2, 0, jnp.where(slot >= 6, 2, jnp.where(slot % 2 == 0, 1, 3)))
        other = jnp.where(slot < 6, jnp.where(slot < 2, slot, jnp.where(slot >= 4, 1, 0)), slot - 6)
        owner = ((x + shift) % 4) * 2 + jnp.where(other == 1, 1 - core, core)
        return owner * 2

    def iteration(turn, carry):
        @pl.when(turn == 1)
        def _():
            to_sibling.wait_recv()

        @pl.when(turn == 2)
        def _():
            to_left.wait_recv()
            pass_left.start()
            share_right.start()

        @pl.when(turn == 3)
        def _():
            to_right.wait_recv()
            pass_right.start()
            share_left.start()

        @pl.when(turn == 4)
        def _():
            share_right.wait_recv()

        @pl.when(turn == 5)
        def _():
            share_left.wait_recv()

        @pl.when(turn == 6)
        def _():
            pass_left.wait_recv()
            pass_right.wait_recv()
            share_far.start()

        @pl.when(turn == 7)
        def _():
            share_far.wait_recv()

        @pl.when(turn < 8)
        def _():
            base = first_block(turn)
            for tree in range(4):
                product = jnp.dot(
                    gathered[turn], weight_here[:, tree * width : (tree + 1) * width],
                    preferred_element_type=jnp.float32,
                ).astype(jnp.bfloat16)
                for side in range(2):
                    block = base + side
                    held[tree, block] = product[side * rows_owned : (side + 1) * rows_owned]
                    direction = TREES[tree][0]

                    @pl.when(bits_of(block)[direction] != my_bits[direction])
                    def _(tree=tree, block=block):
                        tree_message(tree, 0, block)[0].start()

        for step in range(4):
            slot = turn - LAG * (step + 1)

            @pl.when(jnp.logical_and(slot >= 0, slot < 8))
            def _(step=step, slot=slot):
                base = first_block(slot)
                for side in range(2):
                    block = base + side
                    theirs = bits_of(block)
                    for tree in range(4):
                        order = TREES[tree]
                        same = all_of([theirs[d] == my_bits[d] for d in order[: step + 1]])

                        @pl.when(same)
                        def _(tree=tree, block=block, order=order, theirs=theirs):
                            message, index = tree_message(tree, step, block)
                            message.wait_recv()
                            total = held[tree, block].astype(jnp.float32) + inbox[tree, index].astype(jnp.float32)
                            if step == 3:
                                mixed[:, tree * width : (tree + 1) * width] = total.astype(jnp.bfloat16)
                            else:
                                held[tree, block] = total.astype(jnp.bfloat16)
                                onward = order[step + 1]

                                @pl.when(theirs[onward] != my_bits[onward])
                                def _():
                                    tree_message(tree, step + 1, block)[0].start()

        return carry

    lax.fori_loop(0, 8 + 4 * LAG, iteration, 0)

    own_parcel.wait()
    for step in range(1, 8):
        source = (row + 8 - step) % 8
        remote(
            parcels.at[source], arrived.at[source], parcel_send.at[step], parcel_recv.at[source],
            {"row": source, "mp": mp},
        ).wait_recv()
    rows = jnp.concatenate([arrived[block] for block in range(8)], 0)
    slots = lax.broadcasted_iota(jnp.int32, (64, 64), 1).astype(jnp.float32)
    placer = (rows[:, 640:704].astype(jnp.float32) == slots).astype(jnp.bfloat16)
    placed = lax.dot_general(
        placer, rows[:, :640], (((0,), (0,)), ((), ())), preferred_element_type=jnp.float32
    ).astype(jnp.bfloat16)
    for draft in range(5):
        next_kv[draft] = placed[:, draft * 128 : (draft + 1) * 128]

    for copy in (to_left, to_right, to_sibling, pass_left, pass_right, share_right, share_left, share_far):
        copy.wait_send()
    for step in range(1, 8):
        target = (row + step) % 8
        remote(
            parcels.at[target], arrived.at[row], parcel_send.at[step], parcel_recv.at[row],
            {"row": target, "mp": mp},
        ).wait_send()

    def settle(block, carry):
        @pl.when(block != mp)
        def _():
            for tree in range(4):
                remote(
                    held.at[tree, block], inbox.at[tree, 0], tree_send.at[tree, block], tree_recv.at[tree, 0],
                    {"row": row, "mp": along(mp, 0)},
                ).wait_send()

        return carry

    lax.fori_loop(0, 16, settle, 0)


def project(attention, weight, fresh, keyed):
    tokens, depth = attention.shape
    columns = weight.shape[1]
    rows_owned = tokens // 2
    width = columns // 4
    bf16 = jnp.bfloat16
    dma = pltpu.SemaphoreType.DMA
    return pl.pallas_call(
        project_kernel,
        out_shape=(
            jax.ShapeDtypeStruct((rows_owned, columns), bf16),
            jax.ShapeDtypeStruct((5, 64, 128), bf16),
        ),
        in_specs=[
            pl.BlockSpec(memory_space=pl.ANY),
            pl.BlockSpec(memory_space=pl.ANY),
            pl.BlockSpec(memory_space=pltpu.VMEM),
            pl.BlockSpec(memory_space=pltpu.VMEM),
        ],
        out_specs=(pl.BlockSpec(memory_space=pltpu.VMEM), pl.BlockSpec(memory_space=pltpu.VMEM)),
        scratch_shapes=[
            pltpu.VMEM((8, tokens, depth), bf16),
            pltpu.VMEM((depth, columns), bf16),
            pltpu.VMEM((4, 16, rows_owned, width), bf16),
            pltpu.VMEM((4, 15, rows_owned, width), bf16),
            pltpu.VMEM((8, 8, 768), bf16),
            pltpu.VMEM((8, 8, 768), bf16),
            dma((3,)), dma((3,)), dma((5,)), dma((9,)), dma((4, 16)), dma((4, 15)), dma((8,)), dma((8,)),
        ],
        compiler_params=pltpu.CompilerParams(
            collective_id=0, has_side_effects=True, vmem_limit_bytes=56 * 1024 * 1024
        ),
        name="project",
    )(attention, weight, fresh, keyed)


def partner(block, axis, bit):
    count = lax.axis_size(axis)
    route = []
    for low in range(count):
        high = low | 1 << bit
        if high != low and high < count:
            route += [(low, high), (high, low)]
    return lax.ppermute(block, axis, route)


def head_slice(values, start, count):
    return lax.dynamic_slice_in_dim(values, start, count, 3)


def parcel_keys(accepted, dest):
    target = dest // 64
    landing = dest % 64
    beam_index = jnp.arange(64, dtype=jnp.int32)
    earlier = (target[None, :] == target[:, None]) & (beam_index[None, :] < beam_index[:, None])
    position = jnp.sum(earlier.astype(jnp.int32), 1)
    send_slot = target * 8 + position
    order = jnp.arange(8, dtype=jnp.int32)
    draft = jnp.arange(5, dtype=jnp.int32)
    shape = (8, 64, 5)
    slot = jnp.broadcast_to(send_slot[None, :, None], shape)
    on = (order[:, None, None] == draft[None, None, :]) & (draft[None, None, :] < accepted[None, :, None])
    first = (order[:, None, None] == 5) & (draft[None, None, :] == 0)
    keys = jnp.where(on | first, slot, -1)
    keys = jnp.where(order[:, None, None] == 6, landing[None, :, None], keys)
    return keys.reshape(8, 320)


def attend(queries, new_kv, cache_keys, cache_values, cache_lens):
    beams_here = cache_keys.shape[0]
    halves_held = cache_keys.shape[1]
    half_length = cache_keys.shape[2]
    head_size = cache_keys.shape[3]
    drafts = queries.shape[0] // beams_here
    heads_owned = queries.shape[1] // head_size
    mp_place = lax.axis_index("mp")
    lower_side = mp_place % 2 == 0
    partner_queries, partner_fresh = partner((queries, new_kv), "mp", 0)
    group_queries = jnp.where(
        lower_side,
        jnp.concatenate([queries, partner_queries], 1),
        jnp.concatenate([partner_queries, queries], 1),
    )
    fresh_pair = jnp.where(
        lower_side,
        jnp.concatenate([new_kv, partner_fresh], 1),
        jnp.concatenate([partner_fresh, new_kv], 1),
    )
    group_heads = group_queries.shape[1] // head_size
    sides = (mp_place * halves_held + jnp.arange(halves_held, dtype=jnp.int32)) % 2
    query_block = group_queries.reshape(beams_here, drafts, group_heads, head_size)
    fresh_block = fresh_pair.reshape(beams_here, drafts, 2, head_size)
    fresh_keys = fresh_block[:, :, 0]
    fresh_values = fresh_block[:, :, 1]
    scale = head_size ** (-0.5)
    cache_scores = (
        jnp.einsum("btjd,bsid->bstji", query_block, cache_keys, preferred_element_type=jnp.float32)
        * scale
    )
    fresh_scores = (
        jnp.einsum("btjd,bud->btju", query_block, fresh_keys, preferred_element_type=jnp.float32)
        * scale
    )
    spots = sides[:, None] * half_length + jnp.arange(half_length, dtype=jnp.int32)[None, :]
    cache_valid = (spots[None] < cache_lens[:, None, None])[:, :, None, None, :]
    order = jnp.arange(drafts, dtype=jnp.int32)
    fresh_side = (cache_lens[:, None] + order[None, :]) // half_length
    causal = order[:, None] >= order[None, :]
    fresh_valid = (
        causal[None, None] & (fresh_side[:, None, None, :] == sides[None, :, None, None])
    )[:, :, :, None, :]
    cache_masked = jnp.where(cache_valid, cache_scores, masked_score)
    fresh_masked = jnp.where(fresh_valid, fresh_scores[:, None], masked_score)
    highest = jnp.maximum(jnp.max(cache_masked, -1), jnp.max(fresh_masked, -1))
    cache_weights = jnp.where(cache_valid, jnp.exp(cache_masked - highest[..., None]), 0.0).astype(
        jnp.bfloat16
    )
    fresh_weights = jnp.where(fresh_valid, jnp.exp(fresh_masked - highest[..., None]), 0.0).astype(
        jnp.bfloat16
    )
    partial_value = jnp.einsum(
        "bstji,bsid->bstjd", cache_weights, cache_values, preferred_element_type=jnp.float32
    )
    partial_value = partial_value + jnp.einsum(
        "bstju,bud->bstjd", fresh_weights, fresh_values, preferred_element_type=jnp.float32
    )
    weight_mass = jnp.sum(cache_weights.astype(jnp.float32), -1) + jnp.sum(
        fresh_weights.astype(jnp.float32), -1
    )
    own_start = jnp.where(lower_side, 0, heads_owned).astype(jnp.int32)
    other_start = heads_owned - own_start
    got_partial, got_highest, got_mass = partner(
        (
            head_slice(partial_value, other_start, heads_owned),
            head_slice(highest, other_start, heads_owned),
            head_slice(weight_mass, other_start, heads_owned),
        ),
        "mp",
        0,
    )
    own_partial = head_slice(partial_value, own_start, heads_owned)
    own_highest = head_slice(highest, own_start, heads_owned)
    own_mass = head_slice(weight_mass, own_start, heads_owned)
    partial_value = jnp.concatenate([own_partial, got_partial], 1)
    highest = jnp.concatenate([own_highest, got_highest], 1)
    weight_mass = jnp.concatenate([own_mass, got_mass], 1)
    summit = jnp.max(highest, 1)
    factor = jnp.exp(highest - summit[:, None])
    numer = jnp.sum(factor[..., None] * partial_value, 1)
    denom = jnp.sum(factor * weight_mass, 1)
    return (
        (numer / denom[..., None])
        .astype(jnp.bfloat16)
        .reshape(beams_here * drafts, heads_owned * head_size)
    )


def shards(queries, new_kv, cache_keys, cache_values, cache_lens, accepted, dest, out_weight):
    attention = attend(queries, new_kv, cache_keys, cache_values, cache_lens)
    mixed, moved = project(attention, out_weight, new_kv, parcel_keys(accepted, dest))
    return mixed, moved.transpose(1, 0, 2)


def solution(mesh):
    placed = (
        P("row", "mp"),
        P("row", "mp"),
        P("row", "mp", None, None),
        P("row", "mp", None, None),
        P("row"),
        P("row"),
        P("row"),
        P("mp", "row"),
    )
    return jax.shard_map(
        shards,
        mesh=mesh,
        in_specs=placed,
        out_specs=(P("mp", "row"), P("row", None, "mp")),
        check_vma=False,
    )
```

```python
import functools

import jax
import jax.numpy as jnp
from jax import lax
from jax.experimental import pallas as pl
from jax.experimental.pallas import tpu as pltpu
from jax.sharding import PartitionSpec as P

MESH = pl.DeviceIdType.MESH
masked_score = -1e30

TREES = ((0, 2, 1, 3), (2, 1, 3, 0), (1, 3, 0, 2), (3, 0, 2, 1))
STEP_BASE = (0, 8, 12, 14)
LAG = 2


def bits_of(place):
    y, z = place // 4, place % 4
    return (((y + 1) // 2) % 2, y // 2, ((z + 1) // 2) % 2, z // 2)


def along(place, direction):
    y, z = place // 4, place % 4
    if direction == 0:
        y = y + 1 - 2 * (y % 2)
    elif direction == 1:
        y = 3 - y
    elif direction == 2:
        z = z + 1 - 2 * (z % 2)
    else:
        z = 3 - z
    return y * 4 + z


def all_of(terms):
    result = terms[0]
    for term in terms[1:]:
        result = jnp.logical_and(result, term)
    return result

LOG2E = 1.4426950408889634
CHUNKS = 4
UNROLL = 4


def remote(source, target, send_sem, recv_sem, device):
    return pltpu.make_async_remote_copy(
        src_ref=source, dst_ref=target, send_sem=send_sem, recv_sem=recv_sem,
        device_id=device, device_id_type=MESH,
    )


def dot_nt(left, right):
    return lax.dot_general(
        left, right, (((1,), (1,)), ((), ())), preferred_element_type=jnp.float32
    )


def exchange_and_attend(
    lens, queries, fresh, keys, values, side, pair, publish, forward,
    query_rows, query_out, query_in, fresh_in, key_slots, value_slots,
    sum_own, top_own, mass_own, sum_fresh, top_fresh, mass_fresh, part_out, part_in, stat_out, stat_in,
    cache_sem, fresh_sem, query_send, query_recv, part_send, part_recv, stat_send, stat_recv,
):
    beams = keys.shape[0]
    per = beams // CHUNKS
    tokens = per * 5
    span = keys.shape[1]
    scale = 128 ** -0.5 * LOG2E

    def cache_copies(chunk, slot):
        return (
            pltpu.make_async_copy(keys.at[pl.ds(chunk * per, per)], key_slots.at[slot], cache_sem.at[0, slot]),
            pltpu.make_async_copy(values.at[pl.ds(chunk * per, per)], value_slots.at[slot], cache_sem.at[1, slot]),
        )

    def query_message(chunk):
        return remote(query_out.at[chunk], query_in.at[chunk], query_send.at[chunk], query_recv.at[chunk], pair)

    def part_message(chunk):
        return remote(part_out.at[chunk], part_in.at[chunk], part_send.at[chunk], part_recv.at[chunk], pair)

    def stat_message(chunk):
        return remote(stat_out.at[chunk], stat_in.at[chunk], stat_send.at[chunk], stat_recv.at[chunk], pair)

    fresh_message = remote(fresh, fresh_in, fresh_sem.at[0], fresh_sem.at[1], pair)

    def send_query(chunk, carry):
        for head in range(8):
            query_rows[chunk, pl.ds(head, tokens, stride=8), :] = queries[
                pl.ds(chunk * tokens, tokens), head * 128 : (head + 1) * 128
            ].astype(jnp.float32)
        for part in range(per):
            query_out[chunk, part] = query_rows[chunk, part * 40 : part * 40 + 40, :].astype(jnp.bfloat16)
        query_message(chunk).start()

        @pl.when(chunk == 0)
        def _():
            fresh_message.start()

        return carry

    lax.fori_loop(0, CHUNKS, send_query, 0)
    fresh_message.wait_recv()

    rows = per * 40
    row_of = lax.broadcasted_iota(jnp.int32, (rows, tokens), 0)
    key_of = lax.broadcasted_iota(jnp.int32, (rows, tokens), 1)
    fresh_valid = jnp.logical_and(
        row_of // 40 == key_of // 5, (row_of % 40) // 8 >= key_of % 5
    )
    lane = lax.broadcasted_iota(jnp.int32, (40, 128), 1)
    spot = lax.broadcasted_iota(jnp.int32, (80, span), 1) + side * span
    even = side == 0

    def attend_chunk(chunk, carry):
        slot = chunk % 2
        for copy in cache_copies(chunk, slot):
            copy.wait()

        @pl.when(chunk + 1 < CHUNKS)
        def _():
            for copy in cache_copies(chunk + 1, 1 - slot):
                copy.start()

        mine = fresh[pl.ds(chunk * tokens, tokens), :]
        theirs = fresh_in[pl.ds(chunk * tokens, tokens), :]
        fresh_keys = jnp.where(even, mine, theirs)
        fresh_values = jnp.where(even, theirs, mine)
        scores = dot_nt(query_rows[chunk].astype(jnp.bfloat16), fresh_keys)
        scores = jnp.where(fresh_valid, scores, masked_score)
        highest = jnp.max(scores, 1, keepdims=True)
        weights = jnp.exp2((scores - highest) * scale).astype(jnp.bfloat16)
        sums = jnp.dot(
            weights, jnp.concatenate([fresh_values, jnp.ones_like(fresh_values)], 1),
            preferred_element_type=jnp.float32,
        )
        sum_fresh[...] = sums[:, :128]
        mass_fresh[...] = sums[:, 128:]
        top_fresh[...] = jnp.broadcast_to(highest * scale, (rows, 128))

        query_message(chunk).wait_recv()

        def beams_step(group, stat):
            for member in range(UNROLL):
                local = group * UNROLL + member
                at = pl.multiple_of(local * 40, 8)
                block = jnp.concatenate(
                    [
                        query_rows[chunk, pl.ds(at, 40), :],
                        query_in[chunk, local].astype(jnp.float32),
                    ],
                    0,
                ).astype(jnp.bfloat16)
                scores = dot_nt(block, key_slots[slot, local])
                scores = jnp.where(spot < lens[chunk * per + local], scores, masked_score)
                highest = jnp.max(scores, 1, keepdims=True)
                weights = jnp.exp2((scores - highest) * scale).astype(jnp.bfloat16)
                value = value_slots[slot, local]
                sums = jnp.dot(
                    weights, jnp.concatenate([value, jnp.ones_like(value)], 1),
                    preferred_element_type=jnp.float32,
                )
                top = jnp.broadcast_to(highest * scale, (80, 128))
                part_out[chunk, local] = (sums[40:, :128] / sums[40:, 128:]).astype(jnp.bfloat16)
                stat = jnp.where(lane == local, top[40:] + jnp.log2(sums[40:, 128:]), stat)
                near = top_fresh[pl.ds(at, 40), :]
                summit = jnp.maximum(top[:40], near)
                here = jnp.exp2(top[:40] - summit)
                there = jnp.exp2(near - summit)
                sum_own[chunk, pl.ds(at, 40), :] = sums[:40, :128] * here + sum_fresh[pl.ds(at, 40), :] * there
                mass_own[chunk, pl.ds(at, 40), :] = sums[:40, 128:] * here + mass_fresh[pl.ds(at, 40), :] * there
                top_own[chunk, pl.ds(at, 40), :] = summit
            return stat

        stat_out[chunk] = lax.fori_loop(0, per // UNROLL, beams_step, jnp.zeros((40, 128), jnp.float32))
        part_message(chunk).start()
        stat_message(chunk).start()
        return carry

    lax.fori_loop(0, CHUNKS, attend_chunk, 0)

    def combine_chunk(chunk, carry):
        part_message(chunk).wait_recv()
        stat_message(chunk).wait_recv()

        def beams_step(group, inner):
            stat = stat_in[chunk]
            for member in range(UNROLL):
                local = group * UNROLL + member
                at = pl.multiple_of(local * 40, 8)
                other = jnp.sum(jnp.where(lane == local, stat, 0.0), 1, keepdims=True)
                top = top_own[chunk, pl.ds(at, 40), :]
                summit = jnp.maximum(top, other)
                here = jnp.exp2(top - summit)
                there = jnp.exp2(other - summit)
                total = sum_own[chunk, pl.ds(at, 40), :] * here + part_in[chunk, local].astype(jnp.float32) * there
                mass = mass_own[chunk, pl.ds(at, 40), :] * here + there
                sum_fresh[pl.ds(at, 40), :] = total / mass
            return inner

        lax.fori_loop(0, per // UNROLL, beams_step, 0)
        publish(chunk, sum_fresh)
        forward(chunk)
        return carry

    lax.fori_loop(0, CHUNKS, combine_chunk, 0)

    def settle():
        fresh_message.wait_send()

        def one(chunk, carry):
            query_message(chunk).wait_send()
            part_message(chunk).wait_send()
            stat_message(chunk).wait_send()
            return carry

        lax.fori_loop(0, CHUNKS, one, 0)

    return settle


def attention_scratch(beams, span):
    per = beams // CHUNKS
    bf16, f32 = jnp.bfloat16, jnp.float32
    dma = pltpu.SemaphoreType.DMA
    return [
        pltpu.VMEM((CHUNKS, per * 40, 128), f32),
        pltpu.VMEM((CHUNKS, per, 40, 128), bf16),
        pltpu.VMEM((CHUNKS, per, 40, 128), bf16),
        pltpu.VMEM((beams * 5, 128), bf16),
        pltpu.VMEM((2, per, span, 128), bf16),
        pltpu.VMEM((2, per, span, 128), bf16),
        pltpu.VMEM((CHUNKS, per * 40, 128), f32),
        pltpu.VMEM((CHUNKS, per * 40, 128), f32),
        pltpu.VMEM((CHUNKS, per * 40, 128), f32),
        pltpu.VMEM((per * 40, 128), f32),
        pltpu.VMEM((per * 40, 128), f32),
        pltpu.VMEM((per * 40, 128), f32),
        pltpu.VMEM((CHUNKS, per, 40, 128), bf16),
        pltpu.VMEM((CHUNKS, per, 40, 128), bf16),
        pltpu.VMEM((CHUNKS, 40, 128), f32),
        pltpu.VMEM((CHUNKS, 40, 128), f32),
        dma((2, 2)), dma((2,)), dma((CHUNKS,)), dma((CHUNKS,)), dma((CHUNKS,)), dma((CHUNKS,)), dma((CHUNKS,)), dma((CHUNKS,)),
    ]


GATHER_KINDS = (
    "to_right", "to_left", "to_sibling", "share_right", "share_left", "share_far", "pass_left", "pass_right",
)


def step_kernel(
    lens, queries, keys, values, weight, fresh, keyed, mixed, next_kv,
    gathered, weight_here, held, inbox, parcels, arrived,
    local_sem, own_send, far_send, gather_recv, tree_send, tree_recv, parcel_send, parcel_recv, *attention_refs,
):
    row, mp = lax.axis_index("row"), lax.axis_index("mp")
    x, core = row // 2, row % 2
    sibling = {"row": x * 2 + 1 - core, "mp": mp}
    right = {"row": ((x + 1) % 4) * 2 + core, "mp": mp}
    left = {"row": ((x + 3) % 4) * 2 + core, "mp": mp}
    pair = {"row": row, "mp": along(mp, 2)}
    key_slots, value_slots, cache_sem = attention_refs[4], attention_refs[5], attention_refs[16]
    per = keys.shape[0] // CHUNKS
    pltpu.make_async_copy(keys.at[pl.ds(0, per)], key_slots.at[0], cache_sem.at[0, 0]).start()
    pltpu.make_async_copy(values.at[pl.ds(0, per)], value_slots.at[0], cache_sem.at[1, 0]).start()
    weight_copy = pltpu.make_async_copy(weight, weight_here, local_sem.at[0])
    weight_copy.start()

    barrier = pltpu.get_barrier_semaphore()
    for step in range(1, 8):
        pl.semaphore_signal(
            barrier, inc=1, device_id={"row": (row + step) % 8, "mp": mp}, device_id_type=MESH
        )
    for direction in range(4):
        pl.semaphore_signal(
            barrier, inc=1, device_id={"row": row, "mp": along(mp, direction)}, device_id_type=MESH
        )
    pl.semaphore_wait(barrier, 11)

    tokens = gathered.shape[1] // CHUNKS
    half = gathered.shape[2] // 2

    def gather_message(kind, chunk):
        at = pl.ds(pl.multiple_of(chunk * tokens, 8), tokens)
        source, target, device = {
            "to_right": (0, 3, right), "to_left": (0, 2, left), "to_sibling": (0, 1, sibling),
            "share_right": (2, 4, sibling), "share_left": (3, 5, sibling), "share_far": (6, 7, sibling),
            "pass_left": (2, 6, left), "pass_right": (3, 6, right),
        }[kind]
        number = GATHER_KINDS.index(kind)
        send, recv = far_send.at[number, chunk], gather_recv.at[number, chunk]
        if kind == "pass_left":
            part = pl.ds(0, half)
            return remote(gathered.at[2, at, part], gathered.at[6, at, part], send, recv, device)
        if kind == "pass_right":
            part = pl.ds(half, half)
            return remote(gathered.at[3, at, part], gathered.at[6, at, part], send, recv, device)
        return remote(gathered.at[source, at], gathered.at[target, at], send, recv, device)

    def publish(chunk, rows):
        at = pl.ds(pl.multiple_of(chunk * tokens, 8), tokens)
        for head in range(8):
            gathered[0, at, head * 128 : (head + 1) * 128] = rows[pl.ds(head, tokens, stride=8), :].astype(
                jnp.bfloat16
            )
        for kind in ("to_right", "to_left", "to_sibling"):
            gather_message(kind, chunk).start()

    def near(chunk):
        gather_message("to_left", chunk).wait_recv()
        gather_message("pass_left", chunk).start()
        gather_message("share_right", chunk).start()
        gather_message("to_right", chunk).wait_recv()
        gather_message("pass_right", chunk).start()
        gather_message("share_left", chunk).start()

    def far(chunk):
        gather_message("pass_left", chunk).wait_recv()
        gather_message("pass_right", chunk).wait_recv()
        gather_message("share_far", chunk).start()

    def forward(chunk):
        @pl.when(chunk >= 1)
        def _():
            near(chunk - 1)

        @pl.when(chunk >= 2)
        def _():
            far(chunk - 2)

    place = lax.broadcasted_iota(jnp.int32, (64, 320), 0)
    fresh_rows = fresh[...]
    columns = []
    for draft in range(5):
        pick = (keyed[draft : draft + 1, :] == place).astype(jnp.bfloat16)
        columns.append(
            jnp.dot(pick, fresh_rows, preferred_element_type=jnp.float32).astype(jnp.bfloat16)
        )
    label = jnp.sum(
        jnp.where(keyed[5:6, :] == place, keyed[6:7, :], 0).astype(jnp.float32), 1, keepdims=True
    )
    columns.append(jnp.broadcast_to(label, (64, 128)).astype(jnp.bfloat16))
    for block in range(8):
        for part, column in enumerate(columns):
            parcels[block, :, pl.ds(part * 128, 128)] = column[block * 8 : block * 8 + 8]
    own_parcel = pltpu.make_async_copy(parcels.at[row], arrived.at[row], local_sem.at[2])
    own_parcel.start()
    for step in range(1, 8):
        target = (row + step) % 8
        remote(
            parcels.at[target], arrived.at[row], parcel_send.at[step], parcel_recv.at[row],
            {"row": target, "mp": mp},
        ).start()

    settle_attention = exchange_and_attend(
        lens, queries, fresh, keys, values, mp % 2, pair, publish, forward, *attention_refs
    )
    near(CHUNKS - 1)
    far(CHUNKS - 2)
    weight_copy.wait()

    rows_owned = mixed.shape[0]
    width = held.shape[3]
    my_bits = bits_of(mp)

    def tree_message(tree, step, block):
        order = TREES[tree]
        rest = bits_of(block)
        index = STEP_BASE[step]
        for power, direction in enumerate(order[step + 1 :]):
            index = index + rest[direction] * (1 << power)
        return remote(
            held.at[tree, block], inbox.at[tree, index], tree_send.at[tree, block],
            tree_recv.at[tree, index], {"row": row, "mp": along(mp, order[step])},
        ), index

    def first_block(slot):
        shift = jnp.where(slot < 2, 0, jnp.where(slot >= 6, 2, jnp.where(slot % 2 == 0, 1, 3)))
        other = jnp.where(slot < 6, jnp.where(slot < 2, slot, jnp.where(slot >= 4, 1, 0)), slot - 6)
        owner = ((x + shift) % 4) * 2 + jnp.where(other == 1, 1 - core, core)
        return owner * 2

    def iteration(turn, carry):
        def arrive(kind):
            def one(chunk, inner):
                gather_message(kind, chunk).wait_recv()
                return inner

            lax.fori_loop(0, CHUNKS, one, 0)

        @pl.when(turn == 1)
        def _():
            arrive("to_sibling")

        @pl.when(turn == 4)
        def _():
            arrive("share_right")

        @pl.when(turn == 5)
        def _():
            far(CHUNKS - 1)
            arrive("share_left")

        @pl.when(turn == 7)
        def _():
            arrive("share_far")

        @pl.when(turn < 8)
        def _():
            base = first_block(turn)
            for tree in range(4):
                product = jnp.dot(
                    gathered[turn], weight_here[:, tree * width : (tree + 1) * width],
                    preferred_element_type=jnp.float32,
                ).astype(jnp.bfloat16)
                for side in range(2):
                    block = base + side
                    held[tree, block] = product[side * rows_owned : (side + 1) * rows_owned]
                    direction = TREES[tree][0]

                    @pl.when(bits_of(block)[direction] != my_bits[direction])
                    def _(tree=tree, block=block):
                        tree_message(tree, 0, block)[0].start()

        for step in range(4):
            slot = turn - LAG * (step + 1)

            @pl.when(jnp.logical_and(slot >= 0, slot < 8))
            def _(step=step, slot=slot):
                base = first_block(slot)
                for side in range(2):
                    block = base + side
                    theirs = bits_of(block)
                    for tree in range(4):
                        order = TREES[tree]
                        same = all_of([theirs[d] == my_bits[d] for d in order[: step + 1]])

                        @pl.when(same)
                        def _(tree=tree, block=block, order=order, theirs=theirs):
                            message, index = tree_message(tree, step, block)
                            message.wait_recv()
                            total = held[tree, block].astype(jnp.float32) + inbox[tree, index].astype(jnp.float32)
                            if step == 3:
                                mixed[:, tree * width : (tree + 1) * width] = total.astype(jnp.bfloat16)
                            else:
                                held[tree, block] = total.astype(jnp.bfloat16)
                                onward = order[step + 1]

                                @pl.when(theirs[onward] != my_bits[onward])
                                def _():
                                    tree_message(tree, step + 1, block)[0].start()

        return carry

    lax.fori_loop(0, 8 + 4 * LAG, iteration, 0)

    own_parcel.wait()
    for step in range(1, 8):
        source = (row + 8 - step) % 8
        remote(
            parcels.at[source], arrived.at[source], parcel_send.at[step], parcel_recv.at[source],
            {"row": source, "mp": mp},
        ).wait_recv()
    rows = jnp.concatenate([arrived[block] for block in range(8)], 0)
    slots = lax.broadcasted_iota(jnp.int32, (64, 64), 1).astype(jnp.float32)
    placer = (rows[:, 640:704].astype(jnp.float32) == slots).astype(jnp.bfloat16)
    placed = lax.dot_general(
        placer, rows[:, :640], (((0,), (0,)), ((), ())), preferred_element_type=jnp.float32
    ).astype(jnp.bfloat16)
    for draft in range(5):
        next_kv[draft] = placed[:, draft * 128 : (draft + 1) * 128]

    def settle_gather(chunk, carry):
        for kind in GATHER_KINDS:
            gather_message(kind, chunk).wait_send()
        return carry

    lax.fori_loop(0, CHUNKS, settle_gather, 0)
    settle_attention()
    for step in range(1, 8):
        target = (row + step) % 8
        remote(
            parcels.at[target], arrived.at[row], parcel_send.at[step], parcel_recv.at[row],
            {"row": target, "mp": mp},
        ).wait_send()

    def settle(block, carry):
        @pl.when(block != mp)
        def _():
            for tree in range(4):
                remote(
                    held.at[tree, block], inbox.at[tree, 0], tree_send.at[tree, block], tree_recv.at[tree, 0],
                    {"row": row, "mp": along(mp, 0)},
                ).wait_send()

        return carry

    lax.fori_loop(0, 16, settle, 0)


def step(lens, queries, keys, values, weight, fresh, keyed):
    tokens, depth = queries.shape
    columns = weight.shape[1]
    rows_owned = tokens // 2
    width = columns // 4
    bf16 = jnp.bfloat16
    dma = pltpu.SemaphoreType.DMA
    vmem = pl.BlockSpec(memory_space=pltpu.VMEM)
    hbm = pl.BlockSpec(memory_space=pl.ANY)
    return pl.pallas_call(
        step_kernel,
        out_shape=(
            jax.ShapeDtypeStruct((rows_owned, columns), bf16),
            jax.ShapeDtypeStruct((5, 64, 128), bf16),
        ),
        in_specs=[pl.BlockSpec(memory_space=pltpu.SMEM), vmem, hbm, hbm, hbm, vmem, vmem],
        out_specs=(vmem, vmem),
        scratch_shapes=[
            pltpu.VMEM((8, tokens, depth), bf16),
            pltpu.VMEM((depth, columns), bf16),
            pltpu.VMEM((4, 16, rows_owned, width), bf16),
            pltpu.VMEM((4, 15, rows_owned, width), bf16),
            pltpu.VMEM((8, 8, 768), bf16),
            pltpu.VMEM((8, 8, 768), bf16),
            dma((3,)), dma((3,)), dma((8, CHUNKS)), dma((8, CHUNKS)), dma((4, 16)), dma((4, 15)), dma((8,)), dma((8,)),
            *attention_scratch(keys.shape[0], keys.shape[1]),
        ],
        compiler_params=pltpu.CompilerParams(
            collective_id=0, has_side_effects=True, vmem_limit_bytes=60 * 1024 * 1024
        ),
        name="step",
    )(lens, queries, keys, values, weight, fresh, keyed)


def parcel_keys(accepted, dest):
    target = dest // 64
    landing = dest % 64
    beam_index = jnp.arange(64, dtype=jnp.int32)
    earlier = (target[None, :] == target[:, None]) & (beam_index[None, :] < beam_index[:, None])
    position = jnp.sum(earlier.astype(jnp.int32), 1)
    send_slot = target * 8 + position
    order = jnp.arange(8, dtype=jnp.int32)
    draft = jnp.arange(5, dtype=jnp.int32)
    shape = (8, 64, 5)
    slot = jnp.broadcast_to(send_slot[None, :, None], shape)
    on = (order[:, None, None] == draft[None, None, :]) & (draft[None, None, :] < accepted[None, :, None])
    first = (order[:, None, None] == 5) & (draft[None, None, :] == 0)
    keys = jnp.where(on | first, slot, -1)
    keys = jnp.where(order[:, None, None] == 6, landing[None, :, None], keys)
    return keys.reshape(8, 320)


def shards(queries, new_kv, cache_keys, cache_values, cache_lens, accepted, dest, out_weight):
    beams, _, span, size = cache_keys.shape
    mixed, moved = step(
        cache_lens, queries, cache_keys.reshape(beams, span, size), cache_values.reshape(beams, span, size),
        out_weight, new_kv, parcel_keys(accepted, dest),
    )
    return mixed, moved.transpose(1, 0, 2)


def solution(mesh):
    placed = (
        P("row", "mp"),
        P("row", "mp"),
        P("row", "mp", None, None),
        P("row", "mp", None, None),
        P("row"),
        P("row"),
        P("row"),
        P("mp", "row"),
    )
    return jax.shard_map(
        shards,
        mesh=mesh,
        in_specs=placed,
        out_specs=(P("mp", "row"), P("row", None, "mp")),
        check_vma=False,
    )
```

```python
import jax
import jax.numpy as jnp
from jax import lax
from jax.experimental import pallas as pl
from jax.experimental.pallas import tpu as pltpu
from jax.sharding import PartitionSpec as P

MESH = pl.DeviceIdType.MESH
masked_score = -1e30
LOG2E = 1.4426950408889634

TREES = ((0, 2, 1, 3), (2, 1, 3, 0), (1, 3, 0, 2), (3, 0, 2, 1))
WIDTHS = (512, 512, 512, 512)
STARTS = tuple(sum(WIDTHS[:tree]) for tree in range(4))
STEP_BASE = (0, 8, 12, 14)
LAG = 4
FIRST_UNIT = 3
CHUNKS = 4
UNROLL = 4
AHEAD = 2
GATHER_KINDS = (
    "to_right", "to_left", "to_sibling", "share_right", "share_left", "share_far", "pass_left", "pass_right",
)


def bits_of(place):
    y, z = place // 4, place % 4
    return (((y + 1) // 2) % 2, y // 2, ((z + 1) // 2) % 2, z // 2)


def along(place, direction):
    y, z = place // 4, place % 4
    if direction == 0:
        y = y + 1 - 2 * (y % 2)
    elif direction == 1:
        y = 3 - y
    elif direction == 2:
        z = z + 1 - 2 * (z % 2)
    else:
        z = 3 - z
    return y * 4 + z


def all_of(terms):
    result = terms[0]
    for term in terms[1:]:
        result = jnp.logical_and(result, term)
    return result


def within(number, low, high):
    return jnp.logical_and(number >= low, number < high)


def remote(source, target, send_sem, recv_sem, device):
    return pltpu.make_async_remote_copy(
        src_ref=source, dst_ref=target, send_sem=send_sem, recv_sem=recv_sem,
        device_id=device, device_id_type=MESH,
    )


def dot_nt(left, right):
    return lax.dot_general(
        left, right, (((1,), (1,)), ((), ())), preferred_element_type=jnp.float32
    )


def chunk_of(turn):
    return (turn % 2) * 2 + turn // 2


class Attention:
    def __init__(self, lens, queries, fresh, keys, values, side, pair, refs):
        self.lens, self.queries, self.fresh, self.keys, self.values = lens, queries, fresh, keys, values
        self.side, self.pair = side, pair
        (
            self.query_rows, self.query_out, self.query_in, self.fresh_in, self.key_slots, self.value_slots,
            self.sum_own, self.top_own, self.mass_own, self.sum_fresh, self.top_fresh, self.mass_fresh,
            self.part_out, self.part_in, self.stat_out, self.stat_in,
            self.cache_sem, self.fresh_sem, self.query_send, self.query_recv,
            self.part_send, self.part_recv, self.stat_send, self.stat_recv,
        ) = refs
        self.per = keys.shape[0] // CHUNKS
        self.tokens = self.per * 5
        self.span = keys.shape[1]
        self.scale = 128 ** -0.5 * LOG2E

    def cache_copies(self, turn):
        beams = pl.ds(chunk_of(turn) * self.per, self.per)
        slot = turn % 2
        return (
            pltpu.make_async_copy(self.keys.at[beams], self.key_slots.at[slot], self.cache_sem.at[0, slot]),
            pltpu.make_async_copy(self.values.at[beams], self.value_slots.at[slot], self.cache_sem.at[1, slot]),
        )

    def query_message(self, turn):
        return remote(
            self.query_out.at[turn], self.query_in.at[turn], self.query_send.at[turn], self.query_recv.at[turn], self.pair
        )

    def part_message(self, turn):
        return remote(
            self.part_out.at[turn], self.part_in.at[turn], self.part_send.at[turn], self.part_recv.at[turn], self.pair
        )

    def stat_message(self, turn):
        return remote(
            self.stat_out.at[turn], self.stat_in.at[turn], self.stat_send.at[turn], self.stat_recv.at[turn], self.pair
        )

    def fresh_message(self):
        return remote(self.fresh, self.fresh_in, self.fresh_sem.at[0], self.fresh_sem.at[1], self.pair)

    def send_query(self, turn):
        tokens = self.tokens
        at = pl.ds(pl.multiple_of(chunk_of(turn) * tokens, 16), tokens)
        for head in range(8):
            self.query_rows[turn, pl.ds(head, tokens, stride=8), :] = self.queries[
                at, head * 128 : (head + 1) * 128
            ].astype(jnp.float32)
        for part in range(self.per):
            self.query_out[turn, part] = self.query_rows[turn, part * 40 : part * 40 + 40, :].astype(jnp.bfloat16)
        self.query_message(turn).start()

    def attend(self, turn):
        chunk, slot, per = chunk_of(turn), turn % 2, self.per
        tokens, scale = self.tokens, self.scale
        rows = per * 40
        row_of = lax.broadcasted_iota(jnp.int32, (rows, tokens), 0)
        key_of = lax.broadcasted_iota(jnp.int32, (rows, tokens), 1)
        fresh_valid = jnp.logical_and(
            row_of // 40 == key_of // 5, (row_of % 40) // 8 >= key_of % 5
        )
        lane = lax.broadcasted_iota(jnp.int32, (40, 128), 1)
        spot = lax.broadcasted_iota(jnp.int32, (80, self.span), 1) + self.side * self.span

        at = pl.ds(pl.multiple_of(chunk * tokens, 16), tokens)
        mine, theirs = self.fresh[at, :], self.fresh_in[at, :]
        even = self.side == 0
        fresh_keys = jnp.where(even, mine, theirs)
        fresh_values = jnp.where(even, theirs, mine)
        scores = dot_nt(self.query_rows[turn].astype(jnp.bfloat16), fresh_keys)
        scores = jnp.where(fresh_valid, scores, masked_score)
        highest = jnp.max(scores, 1, keepdims=True)
        weights = jnp.exp2((scores - highest) * scale).astype(jnp.bfloat16)
        sums = jnp.dot(
            weights, jnp.concatenate([fresh_values, jnp.ones_like(fresh_values)], 1),
            preferred_element_type=jnp.float32,
        )
        self.sum_fresh[...] = sums[:, :128]
        self.mass_fresh[...] = sums[:, 128:]
        self.top_fresh[...] = jnp.broadcast_to(highest * scale, (rows, 128))

        for copy in self.cache_copies(turn):
            copy.wait()

        @pl.when(turn + 1 < CHUNKS)
        def _():
            for copy in self.cache_copies(turn + 1):
                copy.start()

        self.query_message(turn).wait_recv()

        def beams_step(group, stat):
            for member in range(UNROLL):
                local = group * UNROLL + member
                at = pl.multiple_of(local * 40, 8)
                block = jnp.concatenate(
                    [
                        self.query_rows[turn, pl.ds(at, 40), :],
                        self.query_in[turn, local].astype(jnp.float32),
                    ],
                    0,
                ).astype(jnp.bfloat16)
                scores = dot_nt(block, self.key_slots[slot, local])
                scores = jnp.where(spot < self.lens[chunk * per + local], scores, masked_score)
                highest = jnp.max(scores, 1, keepdims=True)
                weights = jnp.exp2((scores - highest) * scale).astype(jnp.bfloat16)
                value = self.value_slots[slot, local]
                sums = jnp.dot(
                    weights, jnp.concatenate([value, jnp.ones_like(value)], 1),
                    preferred_element_type=jnp.float32,
                )
                top = jnp.broadcast_to(highest * scale, (80, 128))
                self.part_out[turn, local] = (sums[40:, :128] / sums[40:, 128:]).astype(jnp.bfloat16)
                stat = jnp.where(lane == local, top[40:] + jnp.log2(sums[40:, 128:]), stat)
                near = self.top_fresh[pl.ds(at, 40), :]
                summit = jnp.maximum(top[:40], near)
                here = jnp.exp2(top[:40] - summit)
                there = jnp.exp2(near - summit)
                self.sum_own[turn, pl.ds(at, 40), :] = (
                    sums[:40, :128] * here + self.sum_fresh[pl.ds(at, 40), :] * there
                )
                self.mass_own[turn, pl.ds(at, 40), :] = (
                    sums[:40, 128:] * here + self.mass_fresh[pl.ds(at, 40), :] * there
                )
                self.top_own[turn, pl.ds(at, 40), :] = summit
            return stat

        self.stat_out[turn] = lax.fori_loop(0, per // UNROLL, beams_step, jnp.zeros((40, 128), jnp.float32))
        self.part_message(turn).start()
        self.stat_message(turn).start()

    def combine(self, turn):
        self.part_message(turn).wait_recv()
        self.stat_message(turn).wait_recv()
        lane = lax.broadcasted_iota(jnp.int32, (40, 128), 1)

        def beams_step(group, inner):
            stat = self.stat_in[turn]
            for member in range(UNROLL):
                local = group * UNROLL + member
                at = pl.multiple_of(local * 40, 8)
                other = jnp.sum(jnp.where(lane == local, stat, 0.0), 1, keepdims=True)
                top = self.top_own[turn, pl.ds(at, 40), :]
                summit = jnp.maximum(top, other)
                here = jnp.exp2(top - summit)
                there = jnp.exp2(other - summit)
                total = (
                    self.sum_own[turn, pl.ds(at, 40), :] * here + self.part_in[turn, local].astype(jnp.float32) * there
                )
                mass = self.mass_own[turn, pl.ds(at, 40), :] * here + there
                self.sum_fresh[pl.ds(at, 40), :] = total / mass
            return inner

        lax.fori_loop(0, self.per // UNROLL, beams_step, 0)
        return self.sum_fresh

    def settle(self):
        self.fresh_message().wait_send()

        def one(turn, carry):
            self.query_message(turn).wait_send()
            self.part_message(turn).wait_send()
            self.stat_message(turn).wait_send()
            return carry

        lax.fori_loop(0, CHUNKS, one, 0)


def attention_scratch(beams, span):
    per = beams // CHUNKS
    bf16, f32 = jnp.bfloat16, jnp.float32
    dma = pltpu.SemaphoreType.DMA
    return [
        pltpu.VMEM((CHUNKS, per * 40, 128), f32),
        pltpu.VMEM((CHUNKS, per, 40, 128), bf16),
        pltpu.VMEM((CHUNKS, per, 40, 128), bf16),
        pltpu.VMEM((beams * 5, 128), bf16),
        pltpu.VMEM((2, per, span, 128), bf16),
        pltpu.VMEM((2, per, span, 128), bf16),
        pltpu.VMEM((CHUNKS, per * 40, 128), f32),
        pltpu.VMEM((CHUNKS, per * 40, 128), f32),
        pltpu.VMEM((CHUNKS, per * 40, 128), f32),
        pltpu.VMEM((per * 40, 128), f32),
        pltpu.VMEM((per * 40, 128), f32),
        pltpu.VMEM((per * 40, 128), f32),
        pltpu.VMEM((CHUNKS, per, 40, 128), bf16),
        pltpu.VMEM((CHUNKS, per, 40, 128), bf16),
        pltpu.VMEM((CHUNKS, 40, 128), f32),
        pltpu.VMEM((CHUNKS, 40, 128), f32),
        dma((2, 2)), dma((2,)), dma((CHUNKS,)), dma((CHUNKS,)), dma((CHUNKS,)), dma((CHUNKS,)), dma((CHUNKS,)), dma((CHUNKS,)),
    ]


def row_keys(accepted, dest):
    beams = dest.shape[1]
    target = (dest // beams).astype(jnp.float32)
    landing = (dest % beams).astype(jnp.float32)
    over = lax.broadcasted_iota(jnp.int32, (beams, beams), 0)
    lane = lax.broadcasted_iota(jnp.int32, (beams, beams), 1)
    wide = jnp.broadcast_to(target, (beams, beams))
    tall = jnp.sum(jnp.where(over == lane, wide, 0.0), 1, keepdims=True)
    earlier = jnp.logical_and(tall == wide, over < lane)
    position = jnp.sum(jnp.where(earlier, 1.0, 0.0), 0, keepdims=True)
    place = target * (beams // 8) + position
    numbers = jnp.concatenate(
        [place, accepted.astype(jnp.float32), landing, jnp.zeros((5, beams), jnp.float32)], 0
    )
    spread = lax.broadcasted_iota(jnp.int32, (beams, beams * 5), 1) // 5 == lax.broadcasted_iota(
        jnp.int32, (beams, beams * 5), 0
    )
    rows = jnp.dot(
        numbers.astype(jnp.bfloat16), spread.astype(jnp.bfloat16), preferred_element_type=jnp.float32
    )
    return rows[0:1], rows[1:2], rows[2:3]


def step_kernel(
    lens, queries, keys, values, weight, fresh, accepted, dest, mixed, next_kv,
    gathered, weight_here, held_0, held_1, held_2, held_3, inbox_0, inbox_1, inbox_2, inbox_3, parcels, arrived,
    local_sem, far_send, gather_recv, tree_send, tree_recv, parcel_send, parcel_recv, *attention_refs,
):
    row, mp = lax.axis_index("row"), lax.axis_index("mp")
    x, core = row // 2, row % 2
    sibling = {"row": x * 2 + 1 - core, "mp": mp}
    right = {"row": ((x + 1) % 4) * 2 + core, "mp": mp}
    left = {"row": ((x + 3) % 4) * 2 + core, "mp": mp}
    pair = {"row": row, "mp": along(mp, 2)}
    held = (held_0, held_1, held_2, held_3)
    inbox = (inbox_0, inbox_1, inbox_2, inbox_3)
    work = Attention(lens, queries, fresh, keys, values, mp % 2, pair, attention_refs)
    for copy in work.cache_copies(0):
        copy.start()
    weight_copy = pltpu.make_async_copy(weight, weight_here, local_sem.at[0])
    weight_copy.start()

    barrier = pltpu.get_barrier_semaphore()
    for step in range(1, 8):
        pl.semaphore_signal(
            barrier, inc=1, device_id={"row": (row + step) % 8, "mp": mp}, device_id_type=MESH
        )
    for direction in range(4):
        pl.semaphore_signal(
            barrier, inc=1, device_id={"row": row, "mp": along(mp, direction)}, device_id_type=MESH
        )
    pl.semaphore_wait(barrier, 11)

    def send_first(turn, carry):
        work.send_query(turn)

        @pl.when(turn == 0)
        def _():
            work.fresh_message().start()

        return carry

    lax.fori_loop(0, AHEAD, send_first, 0)

    tokens = gathered.shape[2]
    half = gathered.shape[3] // 2

    def gather_message(kind, turn):
        source, target, device = {
            "to_right": (0, 3, right), "to_left": (0, 2, left), "to_sibling": (0, 1, sibling),
            "share_right": (2, 4, sibling), "share_left": (3, 5, sibling), "share_far": (6, 7, sibling),
            "pass_left": (2, 6, left), "pass_right": (3, 6, right),
        }[kind]
        number = GATHER_KINDS.index(kind)
        send, recv = far_send.at[number, turn], gather_recv.at[number, turn]
        if kind in ("pass_left", "pass_right"):
            part = pl.ds(0 if kind == "pass_left" else half, half)
            return remote(
                gathered.at[source, turn, :, part], gathered.at[target, turn, :, part], send, recv, device
            )
        return remote(gathered.at[source, turn], gathered.at[target, turn], send, recv, device)

    def publish(turn, rows):
        for head in range(8):
            gathered[0, turn, :, head * 128 : (head + 1) * 128] = rows[pl.ds(head, tokens, stride=8), :].astype(
                jnp.bfloat16
            )
        for kind in ("to_right", "to_left", "to_sibling"):
            gather_message(kind, turn).start()

    def near(turn):
        gather_message("to_left", turn).wait_recv()
        gather_message("pass_left", turn).start()
        gather_message("share_right", turn).start()
        gather_message("to_right", turn).wait_recv()
        gather_message("pass_right", turn).start()
        gather_message("share_left", turn).start()

    def far(turn):
        gather_message("pass_left", turn).wait_recv()
        gather_message("pass_right", turn).wait_recv()
        gather_message("share_far", turn).start()

    place_row, kept_row, landing_row = row_keys(accepted[...], dest[...])
    place = lax.broadcasted_iota(jnp.int32, (64, 320), 0).astype(jnp.float32)
    draft_of = (lax.broadcasted_iota(jnp.int32, (1, 320), 1) % 5).astype(jnp.float32)
    fresh_rows = fresh[...]
    columns = []
    for draft in range(5):
        taken = jnp.where(jnp.logical_and(draft_of == draft, kept_row > draft), place_row, -1.0)
        columns.append(
            jnp.dot(
                (taken == place).astype(jnp.bfloat16), fresh_rows, preferred_element_type=jnp.float32
            ).astype(jnp.bfloat16)
        )
    first = jnp.where(draft_of == 0, place_row, -1.0)
    label = jnp.sum(jnp.where(first == place, landing_row, 0.0), 1, keepdims=True)
    columns.append(jnp.broadcast_to(label, (64, 128)).astype(jnp.bfloat16))
    for block in range(8):
        for part, column in enumerate(columns):
            parcels[block, :, pl.ds(part * 128, 128)] = column[block * 8 : block * 8 + 8]
    own_parcel = pltpu.make_async_copy(parcels.at[row], arrived.at[row], local_sem.at[1])
    own_parcel.start()
    for step in range(1, 8):
        target = (row + step) % 8
        remote(
            parcels.at[target], arrived.at[row], parcel_send.at[step], parcel_recv.at[row],
            {"row": target, "mp": mp},
        ).start()
    work.fresh_message().wait_recv()
    weight_copy.wait()

    my_bits = bits_of(mp)

    def tree_message(tree, step, phase, block):
        order = TREES[tree]
        rest = bits_of(block)
        index = STEP_BASE[step]
        for power, direction in enumerate(order[step + 1 :]):
            index = index + rest[direction] * (1 << power)
        index = phase * 15 + index
        return remote(
            held[tree].at[phase * 16 + block], inbox[tree].at[index], tree_send.at[tree, phase * 16 + block],
            tree_recv.at[tree, index], {"row": row, "mp": along(mp, order[step])},
        ), index

    def first_block(slot):
        shift = jnp.where(slot < 2, 0, jnp.where(slot >= 6, 2, jnp.where(slot % 2 == 0, 1, 3)))
        other = jnp.where(slot < 6, jnp.where(slot < 2, slot, jnp.where(slot >= 4, 1, 0)), slot - 6)
        owner = ((x + shift) % 4) * 2 + jnp.where(other == 1, 1 - core, core)
        return owner * 2

    def block_of(couple, piece):
        return first_block(couple * 2 + piece // 2) + piece % 2

    def product_unit(unit):
        phase, couple = unit // 4, unit % 4
        early = phase * 2

        @pl.when(couple == 0)
        def _():
            for turn in (early, early + 1):
                gather_message("to_sibling", turn).wait_recv()

        @pl.when(couple == 2)
        def _():
            for turn in (early, early + 1):
                gather_message("share_right", turn).wait_recv()
                gather_message("share_left", turn).wait_recv()

        @pl.when(couple == 3)
        def _():
            for turn in (early, early + 1):
                gather_message("share_far", turn).wait_recv()

        operand = gathered[pl.ds(couple * 2, 2), pl.ds(early, 2)].reshape(4 * tokens, gathered.shape[3])
        for tree in range(4):
            product = jnp.dot(
                operand, weight_here[:, STARTS[tree] : STARTS[tree] + WIDTHS[tree]],
                preferred_element_type=jnp.float32,
            ).astype(jnp.bfloat16)
            direction = TREES[tree][0]
            for piece in range(4):
                block = block_of(couple, piece)
                held[tree][phase * 16 + block] = product[piece * tokens : (piece + 1) * tokens]

                @pl.when(bits_of(block)[direction] != my_bits[direction])
                def _(tree=tree, block=block):
                    tree_message(tree, 0, phase, block)[0].start()

    def receive_unit(step, unit):
        phase, couple = unit // 4, unit % 4

        def one(piece, carry):
            block = block_of(couple, piece)
            theirs = bits_of(block)
            for tree in range(4):
                order = TREES[tree]
                same = all_of([theirs[d] == my_bits[d] for d in order[: step + 1]])

                @pl.when(same)
                def _(tree=tree, order=order):
                    message, index = tree_message(tree, step, phase, block)
                    message.wait_recv()
                    at = phase * 16 + block
                    total = held[tree][at].astype(jnp.float32) + inbox[tree][index].astype(jnp.float32)
                    if step == 3:
                        out = pl.ds(pl.multiple_of(phase * tokens, 16), tokens)
                        mixed[out, STARTS[tree] : STARTS[tree] + WIDTHS[tree]] = total.astype(jnp.bfloat16)
                    else:
                        held[tree][at] = total.astype(jnp.bfloat16)
                        onward = order[step + 1]

                        @pl.when(theirs[onward] != my_bits[onward])
                        def _():
                            tree_message(tree, step + 1, phase, block)[0].start()

            return carry

        lax.fori_loop(0, 4, one, 0)

    def tick(time, carry):
        for step in (3, 2, 1, 0):
            unit = time - FIRST_UNIT - LAG * (step + 1)

            @pl.when(within(unit, 0, 8))
            def _(step=step, unit=unit):
                receive_unit(step, unit)

        @pl.when(within(time - FIRST_UNIT, 0, 8))
        def _():
            product_unit(time - FIRST_UNIT)

        @pl.when(within(time, 0, CHUNKS))
        def _():
            work.attend(time)

            @pl.when(time + AHEAD < CHUNKS)
            def _():
                work.send_query(time + AHEAD)

        @pl.when(within(time - 3, 0, CHUNKS))
        def _():
            far(time - 3)

        @pl.when(within(time - 2, 0, CHUNKS))
        def _():
            near(time - 2)

        @pl.when(within(time - 1, 0, CHUNKS))
        def _():
            publish(time - 1, work.combine(time - 1))

        return carry

    lax.fori_loop(0, FIRST_UNIT + 8 + 4 * LAG, tick, 0)

    own_parcel.wait()
    for step in range(1, 8):
        source = (row + 8 - step) % 8
        remote(
            parcels.at[source], arrived.at[source], parcel_send.at[step], parcel_recv.at[source],
            {"row": source, "mp": mp},
        ).wait_recv()
    rows = jnp.concatenate([arrived[block] for block in range(8)], 0)
    slots = lax.broadcasted_iota(jnp.int32, (64, 64), 1).astype(jnp.float32)
    placer = (rows[:, 640:704].astype(jnp.float32) == slots).astype(jnp.bfloat16)
    placed = lax.dot_general(
        placer, rows[:, :640], (((0,), (0,)), ((), ())), preferred_element_type=jnp.float32
    ).astype(jnp.bfloat16)
    for draft in range(5):
        next_kv[draft] = placed[:, draft * 128 : (draft + 1) * 128]

    def settle_gather(turn, carry):
        for kind in GATHER_KINDS:
            gather_message(kind, turn).wait_send()
        return carry

    lax.fori_loop(0, CHUNKS, settle_gather, 0)
    work.settle()
    for step in range(1, 8):
        target = (row + step) % 8
        remote(
            parcels.at[target], arrived.at[row], parcel_send.at[step], parcel_recv.at[row],
            {"row": target, "mp": mp},
        ).wait_send()

    def settle(block, carry):
        @pl.when(block % 16 != mp)
        def _():
            for tree in range(4):
                remote(
                    held[tree].at[block], inbox[tree].at[0], tree_send.at[tree, block], tree_recv.at[tree, 0],
                    {"row": row, "mp": along(mp, 0)},
                ).wait_send()

        return carry

    lax.fori_loop(0, 32, settle, 0)


def step(lens, queries, keys, values, weight, fresh, accepted, dest):
    tokens, depth = queries.shape
    columns = weight.shape[1]
    beams, span = keys.shape[0], keys.shape[1]
    rows_owned = tokens // 2
    piece = tokens // CHUNKS
    bf16 = jnp.bfloat16
    dma = pltpu.SemaphoreType.DMA
    vmem = pl.BlockSpec(memory_space=pltpu.VMEM)
    hbm = pl.BlockSpec(memory_space=pl.ANY)
    return pl.pallas_call(
        step_kernel,
        out_shape=(
            jax.ShapeDtypeStruct((rows_owned, columns), bf16),
            jax.ShapeDtypeStruct((5, beams, 128), bf16),
        ),
        in_specs=[pl.BlockSpec(memory_space=pltpu.SMEM), vmem, hbm, hbm, hbm, vmem, vmem, vmem],
        out_specs=(vmem, vmem),
        scratch_shapes=[
            pltpu.VMEM((8, CHUNKS, piece, depth), bf16),
            pltpu.VMEM((depth, columns), bf16),
            *[pltpu.VMEM((32, piece, width), bf16) for width in WIDTHS],
            *[pltpu.VMEM((30, piece, width), bf16) for width in WIDTHS],
            pltpu.VMEM((8, 8, 768), bf16),
            pltpu.VMEM((8, 8, 768), bf16),
            dma((2,)), dma((8, CHUNKS)), dma((8, CHUNKS)), dma((4, 32)), dma((4, 30)), dma((8,)), dma((8,)),
            *attention_scratch(beams, span),
        ],
        compiler_params=pltpu.CompilerParams(
            collective_id=0, has_side_effects=True, vmem_limit_bytes=60 * 1024 * 1024
        ),
        name="step",
    )(lens, queries, keys, values, weight, fresh, accepted, dest)


def shards(queries, new_kv, cache_keys, cache_values, cache_lens, accepted, dest, out_weight):
    beams, _, span, size = cache_keys.shape
    mixed, moved = step(
        cache_lens, queries, cache_keys.reshape(beams, span, size), cache_values.reshape(beams, span, size),
        out_weight, new_kv, accepted.reshape(1, beams), dest.reshape(1, beams),
    )
    return mixed, moved.transpose(1, 0, 2)


def solution(mesh):
    placed = (
        P("row", "mp"),
        P("row", "mp"),
        P("row", "mp", None, None),
        P("row", "mp", None, None),
        P("row"),
        P("row"),
        P("row"),
        P("mp", "row"),
    )
    return jax.shard_map(
        shards,
        mesh=mesh,
        in_specs=placed,
        out_specs=(P("mp", "row"), P("row", None, "mp")),
        check_vma=False,
    )
```

```python
import jax
import jax.numpy as jnp
from jax import lax
from jax.experimental import pallas as pl
from jax.experimental.pallas import tpu as pltpu
from jax.sharding import PartitionSpec as P

MESH = pl.DeviceIdType.MESH
masked_score = -1e30
LOG2E = 1.4426950408889634

TREES = ((0, 2, 1, 3), (2, 1, 3, 0), (1, 3, 0, 2), (3, 0, 2, 1))
WIDTHS = (512, 512, 512, 512)
STARTS = tuple(sum(WIDTHS[:tree]) for tree in range(4))
STEP_BASE = (0, 8, 12, 14)
RECEIVES = ((7, 8, 9, 10), (8, 9, 10, 11))
FIRST_UNIT = 3
CHUNKS = 4
UNROLL = 8
AHEAD = 3
BACK = 2
GATHER_KINDS = (
    "to_right", "to_left", "to_sibling", "share_right", "share_left", "share_far", "pass_left", "pass_right",
)


def bits_of(place):
    y, z = place // 4, place % 4
    return (((y + 1) // 2) % 2, y // 2, ((z + 1) // 2) % 2, z // 2)


def along(place, direction):
    y, z = place // 4, place % 4
    if direction == 0:
        y = y + 1 - 2 * (y % 2)
    elif direction == 1:
        y = 3 - y
    elif direction == 2:
        z = z + 1 - 2 * (z % 2)
    else:
        z = 3 - z
    return y * 4 + z


def within(number, low, high):
    return jnp.logical_and(number >= low, number < high)


def remote(source, target, send_sem, recv_sem, device):
    return pltpu.make_async_remote_copy(
        src_ref=source, dst_ref=target, send_sem=send_sem, recv_sem=recv_sem,
        device_id=device, device_id_type=MESH,
    )


def dot_nt(left, right):
    return lax.dot_general(
        left, right, (((1,), (1,)), ((), ())), preferred_element_type=jnp.float32
    )


def chunk_of(turn):
    return (turn % 2) * 2 + turn // 2


class Attention:
    def __init__(self, lens, queries, fresh, keys, values, side, pair, refs):
        self.lens, self.queries, self.fresh, self.keys, self.values = lens, queries, fresh, keys, values
        self.side, self.pair = side, pair
        (
            self.query_rows, self.query_out, self.query_in, self.fresh_in, self.key_slots, self.value_slots,
            self.sum_own, self.top_own, self.mass_own, self.sum_fresh, self.top_fresh, self.mass_fresh,
            self.part_out, self.part_in, self.stat_out, self.stat_in,
            self.cache_sem, self.fresh_sem, self.query_send, self.query_recv,
            self.part_send, self.part_recv, self.stat_send, self.stat_recv,
        ) = refs
        self.per = keys.shape[0] // CHUNKS
        self.tokens = self.per * 5
        self.span = keys.shape[1]
        self.scale = 128 ** -0.5 * LOG2E

    def cache_copies(self, turn):
        beams = pl.ds(chunk_of(turn) * self.per, self.per)
        slot = turn % 2
        return (
            pltpu.make_async_copy(self.keys.at[beams], self.key_slots.at[slot], self.cache_sem.at[0, slot]),
            pltpu.make_async_copy(self.values.at[beams], self.value_slots.at[slot], self.cache_sem.at[1, slot]),
        )

    def query_message(self, turn):
        return remote(
            self.query_out.at[turn], self.query_in.at[turn], self.query_send.at[turn], self.query_recv.at[turn], self.pair
        )

    def part_message(self, turn):
        return remote(
            self.part_out.at[turn], self.part_in.at[turn], self.part_send.at[turn], self.part_recv.at[turn], self.pair
        )

    def stat_message(self, turn):
        return remote(
            self.stat_out.at[turn], self.stat_in.at[turn], self.stat_send.at[turn], self.stat_recv.at[turn], self.pair
        )

    def fresh_message(self):
        return remote(self.fresh, self.fresh_in, self.fresh_sem.at[0], self.fresh_sem.at[1], self.pair)

    def send_query(self, turn):
        tokens = self.tokens
        at = pl.ds(pl.multiple_of(chunk_of(turn) * tokens, 16), tokens)
        for head in range(8):
            self.query_rows[turn, pl.ds(head, tokens, stride=8), :] = self.queries[
                at, head * 128 : (head + 1) * 128
            ].astype(jnp.float32)
        for part in range(self.per):
            self.query_out[turn, part] = self.query_rows[turn, part * 40 : part * 40 + 40, :].astype(jnp.bfloat16)
        self.query_message(turn).start()

    def attend(self, turn):
        chunk, slot, per = chunk_of(turn), turn % 2, self.per
        tokens, scale = self.tokens, self.scale
        rows = per * 40
        row_of = lax.broadcasted_iota(jnp.int32, (rows, tokens), 0)
        key_of = lax.broadcasted_iota(jnp.int32, (rows, tokens), 1)
        fresh_valid = jnp.logical_and(
            row_of // 40 == key_of // 5, (row_of % 40) // 8 >= key_of % 5
        )
        lane = lax.broadcasted_iota(jnp.int32, (40, 128), 1)
        spot = lax.broadcasted_iota(jnp.int32, (80, self.span), 1) + self.side * self.span

        at = pl.ds(pl.multiple_of(chunk * tokens, 16), tokens)
        mine, theirs = self.fresh[at, :], self.fresh_in[at, :]
        even = self.side == 0
        fresh_keys = jnp.where(even, mine, theirs)
        fresh_values = jnp.where(even, theirs, mine)
        scores = dot_nt(self.query_rows[turn].astype(jnp.bfloat16), fresh_keys)
        scores = jnp.where(fresh_valid, scores, masked_score)
        highest = jnp.max(scores, 1, keepdims=True)
        weights = jnp.exp2((scores - highest) * scale).astype(jnp.bfloat16)
        sums = jnp.dot(
            weights, jnp.concatenate([fresh_values, jnp.ones_like(fresh_values)], 1),
            preferred_element_type=jnp.float32,
        )
        self.sum_fresh[...] = sums[:, :128]
        self.mass_fresh[...] = sums[:, 128:]
        self.top_fresh[...] = jnp.broadcast_to(highest * scale, (rows, 128))

        for copy in self.cache_copies(turn):
            copy.wait()

        @pl.when(turn + 1 < CHUNKS)
        def _():
            for copy in self.cache_copies(turn + 1):
                copy.start()

        self.query_message(turn).wait_recv()

        def beams_step(group, stat):
            for member in range(UNROLL):
                local = group * UNROLL + member
                at = pl.multiple_of(local * 40, 8)
                block = jnp.concatenate(
                    [
                        self.query_rows[turn, pl.ds(at, 40), :],
                        self.query_in[turn, local].astype(jnp.float32),
                    ],
                    0,
                ).astype(jnp.bfloat16)
                scores = dot_nt(block, self.key_slots[slot, local])
                scores = jnp.where(spot < self.lens[chunk * per + local], scores, masked_score)
                highest = jnp.max(scores, 1, keepdims=True)
                weights = jnp.exp2((scores - highest) * scale).astype(jnp.bfloat16)
                value = self.value_slots[slot, local]
                sums = jnp.dot(
                    weights, jnp.concatenate([value, jnp.ones_like(value)], 1),
                    preferred_element_type=jnp.float32,
                )
                top = jnp.broadcast_to(highest * scale, (80, 128))
                self.part_out[turn, local] = (sums[40:, :128] / sums[40:, 128:]).astype(jnp.bfloat16)
                stat = jnp.where(lane == local, top[40:] + jnp.log2(sums[40:, 128:]), stat)
                near = self.top_fresh[pl.ds(at, 40), :]
                summit = jnp.maximum(top[:40], near)
                here = jnp.exp2(top[:40] - summit)
                there = jnp.exp2(near - summit)
                self.sum_own[turn, pl.ds(at, 40), :] = (
                    sums[:40, :128] * here + self.sum_fresh[pl.ds(at, 40), :] * there
                )
                self.mass_own[turn, pl.ds(at, 40), :] = (
                    sums[:40, 128:] * here + self.mass_fresh[pl.ds(at, 40), :] * there
                )
                self.top_own[turn, pl.ds(at, 40), :] = summit
            return stat

        self.stat_out[turn] = lax.fori_loop(0, per // UNROLL, beams_step, jnp.zeros((40, 128), jnp.float32))
        self.part_message(turn).start()
        self.stat_message(turn).start()

    def combine(self, turn):
        self.part_message(turn).wait_recv()
        self.stat_message(turn).wait_recv()
        lane = lax.broadcasted_iota(jnp.int32, (40, 128), 1)

        def beams_step(group, inner):
            stat = self.stat_in[turn]
            for member in range(UNROLL):
                local = group * UNROLL + member
                at = pl.multiple_of(local * 40, 8)
                other = jnp.sum(jnp.where(lane == local, stat, 0.0), 1, keepdims=True)
                top = self.top_own[turn, pl.ds(at, 40), :]
                summit = jnp.maximum(top, other)
                here = jnp.exp2(top - summit)
                there = jnp.exp2(other - summit)
                total = (
                    self.sum_own[turn, pl.ds(at, 40), :] * here + self.part_in[turn, local].astype(jnp.float32) * there
                )
                mass = self.mass_own[turn, pl.ds(at, 40), :] * here + there
                self.sum_fresh[pl.ds(at, 40), :] = total / mass
            return inner

        lax.fori_loop(0, self.per // UNROLL, beams_step, 0)
        return self.sum_fresh

    def settle(self):
        self.fresh_message().wait_send()

        def one(turn, carry):
            self.query_message(turn).wait_send()
            self.part_message(turn).wait_send()
            self.stat_message(turn).wait_send()
            return carry

        lax.fori_loop(0, CHUNKS, one, 0)


def attention_scratch(beams, span):
    per = beams // CHUNKS
    bf16, f32 = jnp.bfloat16, jnp.float32
    dma = pltpu.SemaphoreType.DMA
    return [
        pltpu.VMEM((CHUNKS, per * 40, 128), f32),
        pltpu.VMEM((CHUNKS, per, 40, 128), bf16),
        pltpu.VMEM((CHUNKS, per, 40, 128), bf16),
        pltpu.VMEM((beams * 5, 128), bf16),
        pltpu.VMEM((2, per, span, 128), bf16),
        pltpu.VMEM((2, per, span, 128), bf16),
        pltpu.VMEM((CHUNKS, per * 40, 128), f32),
        pltpu.VMEM((CHUNKS, per * 40, 128), f32),
        pltpu.VMEM((CHUNKS, per * 40, 128), f32),
        pltpu.VMEM((per * 40, 128), f32),
        pltpu.VMEM((per * 40, 128), f32),
        pltpu.VMEM((per * 40, 128), f32),
        pltpu.VMEM((CHUNKS, per, 40, 128), bf16),
        pltpu.VMEM((CHUNKS, per, 40, 128), bf16),
        pltpu.VMEM((CHUNKS, 40, 128), f32),
        pltpu.VMEM((CHUNKS, 40, 128), f32),
        dma((2, 2)), dma((2,)), dma((CHUNKS,)), dma((CHUNKS,)), dma((CHUNKS,)), dma((CHUNKS,)), dma((CHUNKS,)), dma((CHUNKS,)),
    ]


def row_keys(accepted, dest):
    beams = dest.shape[1]
    target = (dest // beams).astype(jnp.float32)
    landing = (dest % beams).astype(jnp.float32)
    over = lax.broadcasted_iota(jnp.int32, (beams, beams), 0)
    lane = lax.broadcasted_iota(jnp.int32, (beams, beams), 1)
    wide = jnp.broadcast_to(target, (beams, beams))
    tall = jnp.sum(jnp.where(over == lane, wide, 0.0), 1, keepdims=True)
    earlier = jnp.logical_and(tall == wide, over < lane)
    position = jnp.sum(jnp.where(earlier, 1.0, 0.0), 0, keepdims=True)
    place = target * (beams // 8) + position
    numbers = jnp.concatenate(
        [place, accepted.astype(jnp.float32), landing, jnp.zeros((5, beams), jnp.float32)], 0
    )
    spread = lax.broadcasted_iota(jnp.int32, (beams, beams * 5), 1) // 5 == lax.broadcasted_iota(
        jnp.int32, (beams, beams * 5), 0
    )
    rows = jnp.dot(
        numbers.astype(jnp.bfloat16), spread.astype(jnp.bfloat16), preferred_element_type=jnp.float32
    )
    return rows[0:1], rows[1:2], rows[2:3]


def step_kernel(
    lens, queries, keys, values, weight, fresh, accepted, dest, mixed, next_kv,
    gathered, weight_here, held_0, held_1, held_2, held_3, inbox_0, inbox_1, inbox_2, inbox_3, parcels, arrived,
    local_sem, far_send, gather_recv, tree_send, tree_recv, parcel_send, parcel_recv, *attention_refs,
):
    row, mp = lax.axis_index("row"), lax.axis_index("mp")
    x, core = row // 2, row % 2
    sibling = {"row": x * 2 + 1 - core, "mp": mp}
    right = {"row": ((x + 1) % 4) * 2 + core, "mp": mp}
    left = {"row": ((x + 3) % 4) * 2 + core, "mp": mp}
    pair = {"row": row, "mp": along(mp, 2)}
    held = (held_0, held_1, held_2, held_3)
    inbox = (inbox_0, inbox_1, inbox_2, inbox_3)
    work = Attention(lens, queries, fresh, keys, values, mp % 2, pair, attention_refs)
    for copy in work.cache_copies(0):
        copy.start()
    weight_copy = pltpu.make_async_copy(weight, weight_here, local_sem.at[0])
    weight_copy.start()

    barrier = pltpu.get_barrier_semaphore()
    for step in range(1, 8):
        pl.semaphore_signal(
            barrier, inc=1, device_id={"row": (row + step) % 8, "mp": mp}, device_id_type=MESH
        )
    for direction in range(4):
        pl.semaphore_signal(
            barrier, inc=1, device_id={"row": row, "mp": along(mp, direction)}, device_id_type=MESH
        )
    pl.semaphore_wait(barrier, 11)

    def send_first(turn, carry):
        work.send_query(turn)

        @pl.when(turn == 0)
        def _():
            work.fresh_message().start()

        return carry

    lax.fori_loop(0, AHEAD, send_first, 0)

    tokens = gathered.shape[2]
    half = gathered.shape[3] // 2

    def gather_message(kind, turn):
        source, target, device = {
            "to_right": (0, 3, right), "to_left": (0, 2, left), "to_sibling": (0, 1, sibling),
            "share_right": (2, 4, sibling), "share_left": (3, 5, sibling), "share_far": (6, 7, sibling),
            "pass_left": (2, 6, left), "pass_right": (3, 6, right),
        }[kind]
        number = GATHER_KINDS.index(kind)
        send, recv = far_send.at[number, turn], gather_recv.at[number, turn]
        if kind in ("pass_left", "pass_right"):
            part = pl.ds(0 if kind == "pass_left" else half, half)
            return remote(
                gathered.at[source, turn, :, part], gathered.at[target, turn, :, part], send, recv, device
            )
        return remote(gathered.at[source, turn], gathered.at[target, turn], send, recv, device)

    def publish(turn, rows):
        for head in range(8):
            gathered[0, turn, :, head * 128 : (head + 1) * 128] = rows[pl.ds(head, tokens, stride=8), :].astype(
                jnp.bfloat16
            )
        for kind in ("to_right", "to_left", "to_sibling"):
            gather_message(kind, turn).start()

    def near(turn):
        gather_message("to_left", turn).wait_recv()
        gather_message("pass_left", turn).start()
        gather_message("share_right", turn).start()
        gather_message("to_right", turn).wait_recv()
        gather_message("pass_right", turn).start()
        gather_message("share_left", turn).start()

    def far(turn):
        gather_message("pass_left", turn).wait_recv()
        gather_message("pass_right", turn).wait_recv()
        gather_message("share_far", turn).start()

    place_row, kept_row, landing_row = row_keys(accepted[...], dest[...])
    place = lax.broadcasted_iota(jnp.int32, (64, 320), 0).astype(jnp.float32)
    draft_of = (lax.broadcasted_iota(jnp.int32, (1, 320), 1) % 5).astype(jnp.float32)
    fresh_rows = fresh[...]
    columns = []
    for draft in range(5):
        taken = jnp.where(jnp.logical_and(draft_of == draft, kept_row > draft), place_row, -1.0)
        columns.append(
            jnp.dot(
                (taken == place).astype(jnp.bfloat16), fresh_rows, preferred_element_type=jnp.float32
            ).astype(jnp.bfloat16)
        )
    first = jnp.where(draft_of == 0, place_row, -1.0)
    label = jnp.sum(jnp.where(first == place, landing_row, 0.0), 1, keepdims=True)
    columns.append(jnp.broadcast_to(label, (64, 128)).astype(jnp.bfloat16))
    for block in range(8):
        for part, column in enumerate(columns):
            parcels[block, :, pl.ds(part * 128, 128)] = column[block * 8 : block * 8 + 8]
    own_parcel = pltpu.make_async_copy(parcels.at[row], arrived.at[row], local_sem.at[1])
    own_parcel.start()
    for step in range(1, 8):
        target = (row + step) % 8
        remote(
            parcels.at[target], arrived.at[row], parcel_send.at[step], parcel_recv.at[row],
            {"row": target, "mp": mp},
        ).start()
    work.fresh_message().wait_recv()
    weight_copy.wait()

    my_bits = bits_of(mp)
    y, z = mp // 4, mp % 4
    over_y = (y, along(mp, 0) // 4, along(mp, 1) // 4, (y + 2) % 4)
    over_z = (z, along(mp, 2) % 4, along(mp, 3) % 4, (z + 2) % 4)
    partners = [along(mp, direction) for direction in range(4)]

    def tree_message(tree, step, phase, block, rest):
        index = phase * 15 + STEP_BASE[step] + rest
        return remote(
            held[tree].at[phase * 16 + block], inbox[tree].at[index], tree_send.at[tree, index],
            tree_recv.at[tree, index], {"row": row, "mp": partners[TREES[tree][step]]},
        ), index

    def first_block(slot):
        shift = jnp.where(slot < 2, 0, jnp.where(slot >= 6, 2, jnp.where(slot % 2 == 0, 1, 3)))
        other = jnp.where(slot < 6, jnp.where(slot < 2, slot, jnp.where(slot >= 4, 1, 0)), slot - 6)
        owner = ((x + shift) % 4) * 2 + jnp.where(other == 1, 1 - core, core)
        return owner * 2

    def block_of(couple, piece):
        return first_block(couple * 2 + piece // 2) + piece % 2

    def product_unit(unit):
        phase, couple = unit // 4, unit % 4
        early = phase * 2

        @pl.when(couple == 0)
        def _():
            for turn in (early, early + 1):
                gather_message("to_sibling", turn).wait_recv()

        @pl.when(couple == 2)
        def _():
            for turn in (early, early + 1):
                gather_message("share_right", turn).wait_recv()
                gather_message("share_left", turn).wait_recv()

        @pl.when(couple == 3)
        def _():
            for turn in (early, early + 1):
                gather_message("share_far", turn).wait_recv()

        operand = gathered[pl.ds(couple * 2, 2), pl.ds(early, 2)].reshape(4 * tokens, gathered.shape[3])
        blocks = [block_of(couple, piece) for piece in range(4)]
        across = [[(a + b) % 2 for a, b in zip(bits_of(block), my_bits)] for block in blocks]
        for tree in range(4):
            product = jnp.dot(
                operand, weight_here[:, STARTS[tree] : STARTS[tree] + WIDTHS[tree]],
                preferred_element_type=jnp.float32,
            ).astype(jnp.bfloat16)
            order = TREES[tree]
            for piece in range(4):
                block, apart = blocks[piece], across[piece]
                held[tree][phase * 16 + block] = product[piece * tokens : (piece + 1) * tokens]

                @pl.when(apart[order[0]] == 1)
                def _(tree=tree, block=block, apart=apart, order=order):
                    rest = apart[order[1]] + 2 * apart[order[2]] + 4 * apart[order[3]]
                    tree_message(tree, 0, phase, block, rest)[0].start()

    def receive_step(step, phase):
        count = 1 << (3 - step)
        for rest in sorted(range(count), key=lambda number: (1 - number % 2, number)):
            for tree in range(4):
                apart = [0, 0, 0, 0]
                for later in range(step + 1, 4):
                    apart[TREES[tree][later]] = (rest >> (later - step - 1)) & 1
                block = over_y[apart[0] + 2 * apart[1]] * 4 + over_z[apart[2] + 2 * apart[3]]
                message, index = tree_message(tree, step, phase, block, rest)
                message.wait_recv()
                at = phase * 16 + block
                total = held[tree][at].astype(jnp.float32) + inbox[tree][index].astype(jnp.float32)
                if step == 3:
                    out = pl.ds(pl.multiple_of(phase * tokens, 16), tokens)
                    mixed[out, STARTS[tree] : STARTS[tree] + WIDTHS[tree]] = total.astype(jnp.bfloat16)
                else:
                    held[tree][at] = total.astype(jnp.bfloat16)
                    if rest % 2 == 1:
                        tree_message(tree, step + 1, phase, block, rest // 2)[0].start()

    def tick(time, carry):
        @pl.when(within(time, 0, CHUNKS))
        def _():
            work.attend(time)

            @pl.when(time + AHEAD < CHUNKS)
            def _():
                work.send_query(time + AHEAD)

        @pl.when(within(time - BACK - 2, 0, CHUNKS))
        def _():
            far(time - BACK - 2)

        @pl.when(within(time - BACK - 1, 0, CHUNKS))
        def _():
            near(time - BACK - 1)

        @pl.when(within(time - BACK, 0, CHUNKS))
        def _():
            publish(time - BACK, work.combine(time - BACK))

        @pl.when(within(time - FIRST_UNIT, 0, 8))
        def _():
            product_unit(time - FIRST_UNIT)

        for step in range(4):
            early, late = (FIRST_UNIT + RECEIVES[phase][step] for phase in range(2))

            @pl.when(jnp.logical_or(time == early, time == late))
            def _(step=step, late=late):
                receive_step(step, jnp.where(time == late, 1, 0))

        return carry

    lax.fori_loop(0, FIRST_UNIT + 15, tick, 0)

    own_parcel.wait()
    for step in range(1, 8):
        source = (row + 8 - step) % 8
        remote(
            parcels.at[source], arrived.at[source], parcel_send.at[step], parcel_recv.at[source],
            {"row": source, "mp": mp},
        ).wait_recv()
    rows = jnp.concatenate([arrived[block] for block in range(8)], 0)
    slots = lax.broadcasted_iota(jnp.int32, (64, 64), 1).astype(jnp.float32)
    placer = (rows[:, 640:704].astype(jnp.float32) == slots).astype(jnp.bfloat16)
    placed = lax.dot_general(
        placer, rows[:, :640], (((0,), (0,)), ((), ())), preferred_element_type=jnp.float32
    ).astype(jnp.bfloat16)
    for draft in range(5):
        next_kv[draft] = placed[:, draft * 128 : (draft + 1) * 128]

    def settle_gather(turn, carry):
        for kind in GATHER_KINDS:
            gather_message(kind, turn).wait_send()
        return carry

    lax.fori_loop(0, CHUNKS, settle_gather, 0)
    work.settle()
    for step in range(1, 8):
        target = (row + step) % 8
        remote(
            parcels.at[target], arrived.at[row], parcel_send.at[step], parcel_recv.at[row],
            {"row": target, "mp": mp},
        ).wait_send()

    def settle(index, carry):
        for tree in range(4):
            remote(
                held[tree].at[0], inbox[tree].at[index], tree_send.at[tree, index], tree_recv.at[tree, index],
                {"row": row, "mp": partners[0]},
            ).wait_send()
        return carry

    lax.fori_loop(0, 30, settle, 0)


def step(lens, queries, keys, values, weight, fresh, accepted, dest):
    tokens, depth = queries.shape
    columns = weight.shape[1]
    beams, span = keys.shape[0], keys.shape[1]
    rows_owned = tokens // 2
    piece = tokens // CHUNKS
    bf16 = jnp.bfloat16
    dma = pltpu.SemaphoreType.DMA
    vmem = pl.BlockSpec(memory_space=pltpu.VMEM)
    hbm = pl.BlockSpec(memory_space=pl.ANY)
    return pl.pallas_call(
        step_kernel,
        out_shape=(
            jax.ShapeDtypeStruct((rows_owned, columns), bf16),
            jax.ShapeDtypeStruct((5, beams, 128), bf16),
        ),
        in_specs=[pl.BlockSpec(memory_space=pltpu.SMEM), vmem, hbm, hbm, hbm, vmem, vmem, vmem],
        out_specs=(vmem, vmem),
        scratch_shapes=[
            pltpu.VMEM((8, CHUNKS, piece, depth), bf16),
            pltpu.VMEM((depth, columns), bf16),
            *[pltpu.VMEM((32, piece, width), bf16) for width in WIDTHS],
            *[pltpu.VMEM((30, piece, width), bf16) for width in WIDTHS],
            pltpu.VMEM((8, 8, 768), bf16),
            pltpu.VMEM((8, 8, 768), bf16),
            dma((2,)), dma((8, CHUNKS)), dma((8, CHUNKS)), dma((4, 30)), dma((4, 30)), dma((8,)), dma((8,)),
            *attention_scratch(beams, span),
        ],
        compiler_params=pltpu.CompilerParams(
            collective_id=0, has_side_effects=True, vmem_limit_bytes=60 * 1024 * 1024
        ),
        name="step",
    )(lens, queries, keys, values, weight, fresh, accepted, dest)


def hand_on_kernel(mixed, moved, mixed_out, moved_out):
    mixed_out[...] = mixed[...]
    moved_out[...] = moved[...]


def hand_on(mixed, moved):
    vmem = pl.BlockSpec(memory_space=pltpu.VMEM)
    return pl.pallas_call(
        hand_on_kernel,
        out_shape=(
            jax.ShapeDtypeStruct(mixed.shape, mixed.dtype),
            jax.ShapeDtypeStruct(moved.shape, moved.dtype),
        ),
        in_specs=[vmem, vmem],
        out_specs=(vmem, vmem),
        name="hand_on",
    )(mixed, moved)


def shards(queries, new_kv, cache_keys, cache_values, cache_lens, accepted, dest, out_weight):
    beams, _, span, size = cache_keys.shape
    mixed, moved = step(
        cache_lens, queries, cache_keys.reshape(beams, span, size), cache_values.reshape(beams, span, size),
        out_weight, new_kv, accepted.reshape(1, beams), dest.reshape(1, beams),
    )
    mixed, moved = hand_on(mixed, moved)
    return mixed, moved.transpose(1, 0, 2)


def solution(mesh):
    placed = (
        P("row", "mp"),
        P("row", "mp"),
        P("row", "mp", None, None),
        P("row", "mp", None, None),
        P("row"),
        P("row"),
        P("row"),
        P("mp", "row"),
    )
    return jax.shard_map(
        shards,
        mesh=mesh,
        in_specs=placed,
        out_specs=(P("mp", "row"), P("row", None, "mp")),
        check_vma=False,
    )
```

```python
import jax
import jax.numpy as jnp
from jax import lax
from jax.experimental import pallas as pl
from jax.experimental.pallas import tpu as pltpu
from jax.sharding import PartitionSpec as P

MESH = pl.DeviceIdType.MESH
masked_score = -1e30
LOG2E = 1.4426950408889634

TREES = ((0, 2, 1, 3), (2, 1, 3, 0), (1, 3, 0, 2), (3, 0, 2, 1))
WIDTHS = (512, 512, 512, 512)
STARTS = tuple(sum(WIDTHS[:tree]) for tree in range(4))
STEP_BASE = (0, 8, 12, 14)
WORK = (
    "C0", "C1", "S2", "S3", "K0", "K1", "D0", "N0", "C2", "N1", "F0", "C3",
    "D1", "F1", "D2", "K2", "D3", "K3", "N2", "D4", "N3", "F2", "D5", "F3",
    "D6", "D7", "A0", "B0", "A1", "B1", "A2", "B2", "A3", "B3",
)
CHUNKS = 4
UNROLL = 8
GATHER_KINDS = (
    "to_right", "to_left", "to_sibling", "share_right", "share_left", "share_far", "pass_left", "pass_right",
)


def bits_of(place):
    y, z = place // 4, place % 4
    return (((y + 1) // 2) % 2, y // 2, ((z + 1) // 2) % 2, z // 2)


def along(place, direction):
    y, z = place // 4, place % 4
    if direction == 0:
        y = y + 1 - 2 * (y % 2)
    elif direction == 1:
        y = 3 - y
    elif direction == 2:
        z = z + 1 - 2 * (z % 2)
    else:
        z = 3 - z
    return y * 4 + z


def any_of(terms):
    result = terms[0]
    for term in terms[1:]:
        result = jnp.logical_or(result, term)
    return result


def remote(source, target, send_sem, recv_sem, device):
    return pltpu.make_async_remote_copy(
        src_ref=source, dst_ref=target, send_sem=send_sem, recv_sem=recv_sem,
        device_id=device, device_id_type=MESH,
    )


def dot_nt(left, right):
    return lax.dot_general(
        left, right, (((1,), (1,)), ((), ())), preferred_element_type=jnp.float32
    )


def chunk_of(turn):
    return (turn % 2) * 2 + turn // 2


class Attention:
    def __init__(self, lens, queries, fresh, keys, values, side, pair, refs):
        self.lens, self.queries, self.fresh, self.keys, self.values = lens, queries, fresh, keys, values
        self.side, self.pair = side, pair
        (
            self.query_rows, self.query_out, self.query_in, self.fresh_in, self.key_slots, self.value_slots,
            self.sum_own, self.top_own, self.mass_own, self.sum_fresh, self.top_fresh, self.mass_fresh,
            self.part_out, self.part_in, self.stat_out, self.stat_in,
            self.cache_sem, self.fresh_sem, self.query_send, self.query_recv,
            self.part_send, self.part_recv, self.stat_send, self.stat_recv,
        ) = refs
        self.per = keys.shape[0] // CHUNKS
        self.tokens = self.per * 5
        self.span = keys.shape[1]
        self.scale = 128 ** -0.5 * LOG2E

    def cache_copies(self, turn):
        beams = pl.ds(chunk_of(turn) * self.per, self.per)
        slot = turn % 2
        return (
            pltpu.make_async_copy(self.keys.at[beams], self.key_slots.at[slot], self.cache_sem.at[0, slot]),
            pltpu.make_async_copy(self.values.at[beams], self.value_slots.at[slot], self.cache_sem.at[1, slot]),
        )

    def query_message(self, turn):
        return remote(
            self.query_out.at[turn], self.query_in.at[turn], self.query_send.at[turn], self.query_recv.at[turn], self.pair
        )

    def part_message(self, turn):
        return remote(
            self.part_out.at[turn], self.part_in.at[turn], self.part_send.at[turn], self.part_recv.at[turn], self.pair
        )

    def stat_message(self, turn):
        return remote(
            self.stat_out.at[turn], self.stat_in.at[turn], self.stat_send.at[turn], self.stat_recv.at[turn], self.pair
        )

    def fresh_message(self):
        return remote(self.fresh, self.fresh_in, self.fresh_sem.at[0], self.fresh_sem.at[1], self.pair)

    def send_query(self, turn):
        tokens = self.tokens
        at = pl.ds(pl.multiple_of(chunk_of(turn) * tokens, 16), tokens)
        for head in range(8):
            self.query_rows[turn, pl.ds(head, tokens, stride=8), :] = self.queries[
                at, head * 128 : (head + 1) * 128
            ].astype(jnp.float32)
        for part in range(self.per):
            self.query_out[turn, part] = self.query_rows[turn, part * 40 : part * 40 + 40, :].astype(jnp.bfloat16)
        self.query_message(turn).start()

    def attend(self, turn):
        chunk, slot, per = chunk_of(turn), turn % 2, self.per
        tokens, scale = self.tokens, self.scale
        rows = per * 40
        row_of = lax.broadcasted_iota(jnp.int32, (rows, tokens), 0)
        key_of = lax.broadcasted_iota(jnp.int32, (rows, tokens), 1)
        fresh_valid = jnp.logical_and(
            row_of // 40 == key_of // 5, (row_of % 40) // 8 >= key_of % 5
        )
        lane = lax.broadcasted_iota(jnp.int32, (40, 128), 1)
        spot = lax.broadcasted_iota(jnp.int32, (80, self.span), 1) + self.side * self.span

        at = pl.ds(pl.multiple_of(chunk * tokens, 16), tokens)
        mine, theirs = self.fresh[at, :], self.fresh_in[at, :]
        even = self.side == 0
        fresh_keys = jnp.where(even, mine, theirs)
        fresh_values = jnp.where(even, theirs, mine)
        scores = dot_nt(self.query_rows[turn].astype(jnp.bfloat16), fresh_keys)
        scores = jnp.where(fresh_valid, scores, masked_score)
        highest = jnp.max(scores, 1, keepdims=True)
        weights = jnp.exp2((scores - highest) * scale).astype(jnp.bfloat16)
        sums = jnp.dot(
            weights, jnp.concatenate([fresh_values, jnp.ones_like(fresh_values)], 1),
            preferred_element_type=jnp.float32,
        )
        self.sum_fresh[...] = sums[:, :128]
        self.mass_fresh[...] = sums[:, 128:]
        self.top_fresh[...] = jnp.broadcast_to(highest * scale, (rows, 128))

        for copy in self.cache_copies(turn):
            copy.wait()

        @pl.when(turn + 1 < CHUNKS)
        def _():
            for copy in self.cache_copies(turn + 1):
                copy.start()

        self.query_message(turn).wait_recv()

        def beams_step(group, stat):
            for member in range(UNROLL):
                local = group * UNROLL + member
                at = pl.multiple_of(local * 40, 8)
                block = jnp.concatenate(
                    [
                        self.query_rows[turn, pl.ds(at, 40), :],
                        self.query_in[turn, local].astype(jnp.float32),
                    ],
                    0,
                ).astype(jnp.bfloat16)
                scores = dot_nt(block, self.key_slots[slot, local])
                scores = jnp.where(spot < self.lens[chunk * per + local], scores, masked_score)
                highest = jnp.max(scores, 1, keepdims=True)
                weights = jnp.exp2((scores - highest) * scale).astype(jnp.bfloat16)
                value = self.value_slots[slot, local]
                sums = jnp.dot(
                    weights, jnp.concatenate([value, jnp.ones_like(value)], 1),
                    preferred_element_type=jnp.float32,
                )
                top = jnp.broadcast_to(highest * scale, (80, 128))
                self.part_out[turn, local] = (sums[40:, :128] / sums[40:, 128:]).astype(jnp.bfloat16)
                stat = jnp.where(lane == local, top[40:] + jnp.log2(sums[40:, 128:]), stat)
                near = self.top_fresh[pl.ds(at, 40), :]
                summit = jnp.maximum(top[:40], near)
                here = jnp.exp2(top[:40] - summit)
                there = jnp.exp2(near - summit)
                self.sum_own[turn, pl.ds(at, 40), :] = (
                    sums[:40, :128] * here + self.sum_fresh[pl.ds(at, 40), :] * there
                )
                self.mass_own[turn, pl.ds(at, 40), :] = (
                    sums[:40, 128:] * here + self.mass_fresh[pl.ds(at, 40), :] * there
                )
                self.top_own[turn, pl.ds(at, 40), :] = summit
            return stat

        self.stat_out[turn] = lax.fori_loop(0, per // UNROLL, beams_step, jnp.zeros((40, 128), jnp.float32))
        self.part_message(turn).start()
        self.stat_message(turn).start()

    def combine(self, turn):
        self.part_message(turn).wait_recv()
        self.stat_message(turn).wait_recv()
        lane = lax.broadcasted_iota(jnp.int32, (40, 128), 1)

        def beams_step(group, inner):
            stat = self.stat_in[turn]
            for member in range(UNROLL):
                local = group * UNROLL + member
                at = pl.multiple_of(local * 40, 8)
                other = jnp.sum(jnp.where(lane == local, stat, 0.0), 1, keepdims=True)
                top = self.top_own[turn, pl.ds(at, 40), :]
                summit = jnp.maximum(top, other)
                here = jnp.exp2(top - summit)
                there = jnp.exp2(other - summit)
                total = (
                    self.sum_own[turn, pl.ds(at, 40), :] * here + self.part_in[turn, local].astype(jnp.float32) * there
                )
                mass = self.mass_own[turn, pl.ds(at, 40), :] * here + there
                self.sum_fresh[pl.ds(at, 40), :] = total / mass
            return inner

        lax.fori_loop(0, self.per // UNROLL, beams_step, 0)
        return self.sum_fresh

    def settle(self):
        self.fresh_message().wait_send()

        def one(turn, carry):
            self.query_message(turn).wait_send()
            self.part_message(turn).wait_send()
            self.stat_message(turn).wait_send()
            return carry

        lax.fori_loop(0, CHUNKS, one, 0)


def attention_scratch(beams, span):
    per = beams // CHUNKS
    bf16, f32 = jnp.bfloat16, jnp.float32
    dma = pltpu.SemaphoreType.DMA
    return [
        pltpu.VMEM((CHUNKS, per * 40, 128), f32),
        pltpu.VMEM((CHUNKS, per, 40, 128), bf16),
        pltpu.VMEM((CHUNKS, per, 40, 128), bf16),
        pltpu.VMEM((beams * 5, 128), bf16),
        pltpu.VMEM((2, per, span, 128), bf16),
        pltpu.VMEM((2, per, span, 128), bf16),
        pltpu.VMEM((CHUNKS, per * 40, 128), f32),
        pltpu.VMEM((CHUNKS, per * 40, 128), f32),
        pltpu.VMEM((CHUNKS, per * 40, 128), f32),
        pltpu.VMEM((per * 40, 128), f32),
        pltpu.VMEM((per * 40, 128), f32),
        pltpu.VMEM((per * 40, 128), f32),
        pltpu.VMEM((CHUNKS, per, 40, 128), bf16),
        pltpu.VMEM((CHUNKS, per, 40, 128), bf16),
        pltpu.VMEM((CHUNKS, 40, 128), f32),
        pltpu.VMEM((CHUNKS, 40, 128), f32),
        dma((2, 2)), dma((2,)), dma((CHUNKS,)), dma((CHUNKS,)), dma((CHUNKS,)), dma((CHUNKS,)), dma((CHUNKS,)), dma((CHUNKS,)),
    ]


def row_keys(accepted, dest):
    beams = dest.shape[1]
    target = (dest // beams).astype(jnp.float32)
    landing = (dest % beams).astype(jnp.float32)
    over = lax.broadcasted_iota(jnp.int32, (beams, beams), 0)
    lane = lax.broadcasted_iota(jnp.int32, (beams, beams), 1)
    wide = jnp.broadcast_to(target, (beams, beams))
    tall = jnp.sum(jnp.where(over == lane, wide, 0.0), 1, keepdims=True)
    earlier = jnp.logical_and(tall == wide, over < lane)
    position = jnp.sum(jnp.where(earlier, 1.0, 0.0), 0, keepdims=True)
    place = target * (beams // 8) + position
    numbers = jnp.concatenate(
        [place, accepted.astype(jnp.float32), landing, jnp.zeros((5, beams), jnp.float32)], 0
    )
    spread = lax.broadcasted_iota(jnp.int32, (beams, beams * 5), 1) // 5 == lax.broadcasted_iota(
        jnp.int32, (beams, beams * 5), 0
    )
    rows = jnp.dot(
        numbers.astype(jnp.bfloat16), spread.astype(jnp.bfloat16), preferred_element_type=jnp.float32
    )
    return rows[0:1], rows[1:2], rows[2:3]


def step_kernel(
    lens, queries, keys, values, weight, fresh, accepted, dest, mixed, next_kv,
    gathered, weight_here, held_0, held_1, held_2, held_3, inbox_0, inbox_1, inbox_2, inbox_3, parcels, arrived,
    local_sem, far_send, gather_recv, tree_send, tree_recv, parcel_send, parcel_recv, *attention_refs,
):
    row, mp = lax.axis_index("row"), lax.axis_index("mp")
    x, core = row // 2, row % 2
    sibling = {"row": x * 2 + 1 - core, "mp": mp}
    right = {"row": ((x + 1) % 4) * 2 + core, "mp": mp}
    left = {"row": ((x + 3) % 4) * 2 + core, "mp": mp}
    pair = {"row": row, "mp": along(mp, 2)}
    held = (held_0, held_1, held_2, held_3)
    inbox = (inbox_0, inbox_1, inbox_2, inbox_3)
    work = Attention(lens, queries, fresh, keys, values, mp % 2, pair, attention_refs)
    for copy in work.cache_copies(0):
        copy.start()
    weight_copy = pltpu.make_async_copy(weight, weight_here, local_sem.at[0])
    weight_copy.start()

    barrier = pltpu.get_barrier_semaphore()
    for step in range(1, 8):
        pl.semaphore_signal(
            barrier, inc=1, device_id={"row": (row + step) % 8, "mp": mp}, device_id_type=MESH
        )
    for direction in range(4):
        pl.semaphore_signal(
            barrier, inc=1, device_id={"row": row, "mp": along(mp, direction)}, device_id_type=MESH
        )
    pl.semaphore_wait(barrier, 11)

    def send_first(turn, carry):
        work.send_query(turn)

        @pl.when(turn == 0)
        def _():
            work.fresh_message().start()

        return carry

    lax.fori_loop(0, 2, send_first, 0)

    tokens = gathered.shape[2]
    half = gathered.shape[3] // 2

    def gather_message(kind, turn):
        source, target, device = {
            "to_right": (0, 3, right), "to_left": (0, 2, left), "to_sibling": (0, 1, sibling),
            "share_right": (2, 4, sibling), "share_left": (3, 5, sibling), "share_far": (6, 7, sibling),
            "pass_left": (2, 6, left), "pass_right": (3, 6, right),
        }[kind]
        number = GATHER_KINDS.index(kind)
        send, recv = far_send.at[number, turn], gather_recv.at[number, turn]
        if kind in ("pass_left", "pass_right"):
            part = pl.ds(0 if kind == "pass_left" else half, half)
            return remote(
                gathered.at[source, turn, :, part], gathered.at[target, turn, :, part], send, recv, device
            )
        return remote(gathered.at[source, turn], gathered.at[target, turn], send, recv, device)

    def publish(turn, rows):
        for head in range(8):
            gathered[0, turn, :, head * 128 : (head + 1) * 128] = rows[pl.ds(head, tokens, stride=8), :].astype(
                jnp.bfloat16
            )
        for kind in ("to_right", "to_left", "to_sibling"):
            gather_message(kind, turn).start()

    def near(turn):
        gather_message("to_left", turn).wait_recv()
        gather_message("pass_left", turn).start()
        gather_message("share_right", turn).start()
        gather_message("to_right", turn).wait_recv()
        gather_message("pass_right", turn).start()
        gather_message("share_left", turn).start()

    def far(turn):
        gather_message("pass_left", turn).wait_recv()
        gather_message("pass_right", turn).wait_recv()
        gather_message("share_far", turn).start()

    place_row, kept_row, landing_row = row_keys(accepted[...], dest[...])
    place = lax.broadcasted_iota(jnp.int32, (64, 320), 0).astype(jnp.float32)
    draft_of = (lax.broadcasted_iota(jnp.int32, (1, 320), 1) % 5).astype(jnp.float32)
    fresh_rows = fresh[...]
    columns = []
    for draft in range(5):
        taken = jnp.where(jnp.logical_and(draft_of == draft, kept_row > draft), place_row, -1.0)
        columns.append(
            jnp.dot(
                (taken == place).astype(jnp.bfloat16), fresh_rows, preferred_element_type=jnp.float32
            ).astype(jnp.bfloat16)
        )
    first = jnp.where(draft_of == 0, place_row, -1.0)
    label = jnp.sum(jnp.where(first == place, landing_row, 0.0), 1, keepdims=True)
    columns.append(jnp.broadcast_to(label, (64, 128)).astype(jnp.bfloat16))
    for block in range(8):
        for part, column in enumerate(columns):
            parcels[block, :, pl.ds(part * 128, 128)] = column[block * 8 : block * 8 + 8]
    own_parcel = pltpu.make_async_copy(parcels.at[row], arrived.at[row], local_sem.at[1])
    own_parcel.start()
    for step in range(1, 8):
        target = (row + step) % 8
        remote(
            parcels.at[target], arrived.at[row], parcel_send.at[step], parcel_recv.at[row],
            {"row": target, "mp": mp},
        ).start()
    work.fresh_message().wait_recv()
    weight_copy.wait()

    my_bits = bits_of(mp)
    y, z = mp // 4, mp % 4
    over_y = (y, along(mp, 0) // 4, along(mp, 1) // 4, (y + 2) % 4)
    over_z = (z, along(mp, 2) % 4, along(mp, 3) % 4, (z + 2) % 4)
    partners = [along(mp, direction) for direction in range(4)]

    def tree_message(tree, step, phase, block, rest):
        index = phase * 15 + STEP_BASE[step] + rest
        return remote(
            held[tree].at[phase * 16 + block], inbox[tree].at[index], tree_send.at[tree, index],
            tree_recv.at[tree, index], {"row": row, "mp": partners[TREES[tree][step]]},
        ), index

    def first_block(slot):
        shift = jnp.where(slot < 2, 0, jnp.where(slot >= 6, 2, jnp.where(slot % 2 == 0, 1, 3)))
        other = jnp.where(slot < 6, jnp.where(slot < 2, slot, jnp.where(slot >= 4, 1, 0)), slot - 6)
        owner = ((x + shift) % 4) * 2 + jnp.where(other == 1, 1 - core, core)
        return owner * 2

    def block_of(couple, piece):
        return first_block(couple * 2 + piece // 2) + piece % 2

    def product_unit(unit):
        phase, couple = unit // 4, unit % 4
        early = phase * 2

        @pl.when(couple == 0)
        def _():
            for turn in (early, early + 1):
                gather_message("to_sibling", turn).wait_recv()

        @pl.when(couple == 2)
        def _():
            for turn in (early, early + 1):
                gather_message("share_right", turn).wait_recv()
                gather_message("share_left", turn).wait_recv()

        @pl.when(couple == 3)
        def _():
            for turn in (early, early + 1):
                gather_message("share_far", turn).wait_recv()

        operand = gathered[pl.ds(couple * 2, 2), pl.ds(early, 2)].reshape(4 * tokens, gathered.shape[3])
        blocks = [block_of(couple, piece) for piece in range(4)]
        across = [[(a + b) % 2 for a, b in zip(bits_of(block), my_bits)] for block in blocks]
        for tree in range(4):
            product = jnp.dot(
                operand, weight_here[:, STARTS[tree] : STARTS[tree] + WIDTHS[tree]],
                preferred_element_type=jnp.float32,
            ).astype(jnp.bfloat16)
            order = TREES[tree]
            for piece in range(4):
                block, apart = blocks[piece], across[piece]
                held[tree][phase * 16 + block] = product[piece * tokens : (piece + 1) * tokens]

                @pl.when(apart[order[0]] == 1)
                def _(tree=tree, block=block, apart=apart, order=order):
                    rest = apart[order[1]] + 2 * apart[order[2]] + 4 * apart[order[3]]
                    tree_message(tree, 0, phase, block, rest)[0].start()

    def receive_step(step, phase):
        count = 1 << (3 - step)
        for rest in sorted(range(count), key=lambda number: (1 - number % 2, number)):
            for tree in range(4):
                apart = [0, 0, 0, 0]
                for later in range(step + 1, 4):
                    apart[TREES[tree][later]] = (rest >> (later - step - 1)) & 1
                block = over_y[apart[0] + 2 * apart[1]] * 4 + over_z[apart[2] + 2 * apart[3]]
                message, index = tree_message(tree, step, phase, block, rest)
                message.wait_recv()
                at = phase * 16 + block
                total = held[tree][at].astype(jnp.float32) + inbox[tree][index].astype(jnp.float32)
                if step == 3:
                    out = pl.ds(pl.multiple_of(phase * tokens, 16), tokens)
                    mixed[out, STARTS[tree] : STARTS[tree] + WIDTHS[tree]] = total.astype(jnp.bfloat16)
                else:
                    held[tree][at] = total.astype(jnp.bfloat16)
                    if rest % 2 == 1:
                        tree_message(tree, step + 1, phase, block, rest // 2)[0].start()

    actions = {
        "S": work.send_query,
        "C": work.attend,
        "K": lambda turn: publish(turn, work.combine(turn)),
        "N": near,
        "F": far,
        "D": product_unit,
    }

    def tick(time, carry):
        for kind, action in actions.items():
            spots = [(spot, int(name[1])) for spot, name in enumerate(WORK) if name[0] == kind]

            @pl.when(any_of([time == spot for spot, _ in spots]))
            def _(action=action, spots=spots):
                action(sum(jnp.where(time == spot, number, 0) for spot, number in spots))

        for step in range(4):
            early, late = WORK.index(f"A{step}"), WORK.index(f"B{step}")

            @pl.when(jnp.logical_or(time == early, time == late))
            def _(step=step, late=late):
                receive_step(step, jnp.where(time == late, 1, 0))

        return carry

    lax.fori_loop(0, len(WORK), tick, 0)

    own_parcel.wait()
    for step in range(1, 8):
        source = (row + 8 - step) % 8
        remote(
            parcels.at[source], arrived.at[source], parcel_send.at[step], parcel_recv.at[source],
            {"row": source, "mp": mp},
        ).wait_recv()
    rows = jnp.concatenate([arrived[block] for block in range(8)], 0)
    slots = lax.broadcasted_iota(jnp.int32, (64, 64), 1).astype(jnp.float32)
    placer = (rows[:, 640:704].astype(jnp.float32) == slots).astype(jnp.bfloat16)
    placed = lax.dot_general(
        placer, rows[:, :640], (((0,), (0,)), ((), ())), preferred_element_type=jnp.float32
    ).astype(jnp.bfloat16)
    for draft in range(5):
        next_kv[draft] = placed[:, draft * 128 : (draft + 1) * 128]

    def settle_gather(turn, carry):
        for kind in GATHER_KINDS:
            gather_message(kind, turn).wait_send()
        return carry

    lax.fori_loop(0, CHUNKS, settle_gather, 0)
    work.settle()
    for step in range(1, 8):
        target = (row + step) % 8
        remote(
            parcels.at[target], arrived.at[row], parcel_send.at[step], parcel_recv.at[row],
            {"row": target, "mp": mp},
        ).wait_send()

    def settle(index, carry):
        for tree in range(4):
            remote(
                held[tree].at[0], inbox[tree].at[index], tree_send.at[tree, index], tree_recv.at[tree, index],
                {"row": row, "mp": partners[0]},
            ).wait_send()
        return carry

    lax.fori_loop(0, 30, settle, 0)


def step(lens, queries, keys, values, weight, fresh, accepted, dest):
    tokens, depth = queries.shape
    columns = weight.shape[1]
    beams, span = keys.shape[0], keys.shape[1]
    rows_owned = tokens // 2
    piece = tokens // CHUNKS
    bf16 = jnp.bfloat16
    dma = pltpu.SemaphoreType.DMA
    vmem = pl.BlockSpec(memory_space=pltpu.VMEM)
    hbm = pl.BlockSpec(memory_space=pl.ANY)
    return pl.pallas_call(
        step_kernel,
        out_shape=(
            jax.ShapeDtypeStruct((rows_owned, columns), bf16),
            jax.ShapeDtypeStruct((5, beams, 128), bf16),
        ),
        in_specs=[pl.BlockSpec(memory_space=pltpu.SMEM), vmem, hbm, hbm, hbm, vmem, vmem, vmem],
        out_specs=(vmem, vmem),
        scratch_shapes=[
            pltpu.VMEM((8, CHUNKS, piece, depth), bf16),
            pltpu.VMEM((depth, columns), bf16),
            *[pltpu.VMEM((32, piece, width), bf16) for width in WIDTHS],
            *[pltpu.VMEM((30, piece, width), bf16) for width in WIDTHS],
            pltpu.VMEM((8, 8, 768), bf16),
            pltpu.VMEM((8, 8, 768), bf16),
            dma((2,)), dma((8, CHUNKS)), dma((8, CHUNKS)), dma((4, 30)), dma((4, 30)), dma((8,)), dma((8,)),
            *attention_scratch(beams, span),
        ],
        compiler_params=pltpu.CompilerParams(
            collective_id=0, has_side_effects=True, vmem_limit_bytes=60 * 1024 * 1024
        ),
        name="step",
    )(lens, queries, keys, values, weight, fresh, accepted, dest)


def hand_on_kernel(mixed, moved, mixed_out, moved_out):
    mixed_out[...] = mixed[...]
    moved_out[...] = moved[...]


def hand_on(mixed, moved):
    vmem = pl.BlockSpec(memory_space=pltpu.VMEM)
    return pl.pallas_call(
        hand_on_kernel,
        out_shape=(
            jax.ShapeDtypeStruct(mixed.shape, mixed.dtype),
            jax.ShapeDtypeStruct(moved.shape, moved.dtype),
        ),
        in_specs=[vmem, vmem],
        out_specs=(vmem, vmem),
        name="hand_on",
    )(mixed, moved)


def shards(queries, new_kv, cache_keys, cache_values, cache_lens, accepted, dest, out_weight):
    beams, _, span, size = cache_keys.shape
    mixed, moved = step(
        cache_lens, queries, cache_keys.reshape(beams, span, size), cache_values.reshape(beams, span, size),
        out_weight, new_kv, accepted.reshape(1, beams), dest.reshape(1, beams),
    )
    mixed, moved = hand_on(mixed, moved)
    return mixed, moved.transpose(1, 0, 2)


def solution(mesh):
    placed = (
        P("row", "mp"),
        P("row", "mp"),
        P("row", "mp", None, None),
        P("row", "mp", None, None),
        P("row"),
        P("row"),
        P("row"),
        P("mp", "row"),
    )
    return jax.shard_map(
        shards,
        mesh=mesh,
        in_specs=placed,
        out_specs=(P("mp", "row"), P("row", None, "mp")),
        check_vma=False,
    )
```

```python
import jax
import jax.numpy as jnp
from jax import lax
from jax.experimental import pallas as pl
from jax.experimental.pallas import tpu as pltpu
from jax.sharding import PartitionSpec as P

MESH = pl.DeviceIdType.MESH
masked_score = -1e30
LOG2E = 1.4426950408889634

TREES = ((0, 2, 1, 3), (2, 1, 3, 0), (1, 3, 0, 2), (3, 0, 2, 1))
WIDTHS = (512, 512, 512, 512)
STARTS = tuple(sum(WIDTHS[:tree]) for tree in range(4))
STEP_BASE = (0, 8, 12, 14)
WORK = (
    "C0", "C1", "S2", "S3", "K0", "K1", "D0", "N0", "C2", "N1", "F0", "C3",
    "D1", "F1", "D2", "K2", "D3", "K3", "N2", "D4", "N3", "F2", "D5", "F3",
    "D6", "D7", "A0", "B0", "A1", "B1", "A2", "B2", "A3", "B3",
)
CHUNKS = 4
UNROLL = 8
GATHER_KINDS = (
    "to_right", "to_left", "to_sibling", "share_right", "share_left", "share_far", "pass_left", "pass_right",
)


def bits_of(place):
    y, z = place // 4, place % 4
    return (((y + 1) // 2) % 2, y // 2, ((z + 1) // 2) % 2, z // 2)


def along(place, direction):
    y, z = place // 4, place % 4
    if direction == 0:
        y = y + 1 - 2 * (y % 2)
    elif direction == 1:
        y = 3 - y
    elif direction == 2:
        z = z + 1 - 2 * (z % 2)
    else:
        z = 3 - z
    return y * 4 + z


def any_of(terms):
    result = terms[0]
    for term in terms[1:]:
        result = jnp.logical_or(result, term)
    return result


def remote(source, target, send_sem, recv_sem, device):
    return pltpu.make_async_remote_copy(
        src_ref=source, dst_ref=target, send_sem=send_sem, recv_sem=recv_sem,
        device_id=device, device_id_type=MESH,
    )


def dot_nt(left, right):
    return lax.dot_general(
        left, right, (((1,), (1,)), ((), ())), preferred_element_type=jnp.float32
    )


def chunk_of(turn):
    return (turn % 2) * 2 + turn // 2


class Attention:
    def __init__(self, lens, queries, fresh, keys, values, side, pair, refs):
        self.lens, self.queries, self.fresh, self.keys, self.values = lens, queries, fresh, keys, values
        self.side, self.pair = side, pair
        (
            self.query_rows, self.query_out, self.query_in, self.fresh_in, self.key_slots, self.value_slots,
            self.sum_own, self.top_own, self.mass_own, self.sum_fresh, self.top_fresh, self.mass_fresh,
            self.part_out, self.part_in, self.stat_out, self.stat_in,
            self.cache_sem, self.fresh_sem, self.query_send, self.query_recv,
            self.part_send, self.part_recv, self.stat_send, self.stat_recv,
        ) = refs
        self.per = keys.shape[0] // CHUNKS
        self.tokens = self.per * 5
        self.span = keys.shape[1]
        self.scale = 128 ** -0.5 * LOG2E

    def cache_copies(self, turn):
        beams = pl.ds(chunk_of(turn) * self.per, self.per)
        slot = turn % 2
        return (
            pltpu.make_async_copy(self.keys.at[beams], self.key_slots.at[slot], self.cache_sem.at[0, slot]),
            pltpu.make_async_copy(self.values.at[beams], self.value_slots.at[slot], self.cache_sem.at[1, slot]),
        )

    def query_message(self, turn):
        return remote(
            self.query_out.at[turn], self.query_in.at[turn], self.query_send.at[turn], self.query_recv.at[turn], self.pair
        )

    def part_message(self, turn):
        return remote(
            self.part_out.at[turn], self.part_in.at[turn], self.part_send.at[turn], self.part_recv.at[turn], self.pair
        )

    def stat_message(self, turn):
        return remote(
            self.stat_out.at[turn], self.stat_in.at[turn], self.stat_send.at[turn], self.stat_recv.at[turn], self.pair
        )

    def fresh_message(self):
        return remote(self.fresh, self.fresh_in, self.fresh_sem.at[0], self.fresh_sem.at[1], self.pair)

    def send_query(self, turn):
        tokens = self.tokens
        at = pl.ds(pl.multiple_of(chunk_of(turn) * tokens, 16), tokens)
        for head in range(8):
            self.query_rows[turn, pl.ds(head, tokens, stride=8), :] = self.queries[
                at, head * 128 : (head + 1) * 128
            ].astype(jnp.float32)
        for part in range(self.per):
            self.query_out[turn, part] = self.query_rows[turn, part * 40 : part * 40 + 40, :].astype(jnp.bfloat16)
        self.query_message(turn).start()

    def attend(self, turn):
        chunk, slot, per = chunk_of(turn), turn % 2, self.per
        tokens, scale = self.tokens, self.scale
        rows = per * 40
        row_of = lax.broadcasted_iota(jnp.int32, (rows, tokens), 0)
        key_of = lax.broadcasted_iota(jnp.int32, (rows, tokens), 1)
        fresh_valid = jnp.logical_and(
            row_of // 40 == key_of // 5, (row_of % 40) // 8 >= key_of % 5
        )
        lane = lax.broadcasted_iota(jnp.int32, (40, 128), 1)
        spot = lax.broadcasted_iota(jnp.int32, (80, self.span), 1) + self.side * self.span

        at = pl.ds(pl.multiple_of(chunk * tokens, 16), tokens)
        mine, theirs = self.fresh[at, :], self.fresh_in[at, :]
        even = self.side == 0
        fresh_keys = jnp.where(even, mine, theirs)
        fresh_values = jnp.where(even, theirs, mine)
        scores = dot_nt(self.query_rows[turn, :rows, :].astype(jnp.bfloat16), fresh_keys)
        scores = jnp.where(fresh_valid, scores, masked_score)
        highest = jnp.max(scores, 1, keepdims=True)
        weights = jnp.exp2((scores - highest) * scale).astype(jnp.bfloat16)
        sums = jnp.dot(
            weights, jnp.concatenate([fresh_values, jnp.ones_like(fresh_values)], 1),
            preferred_element_type=jnp.float32,
        )
        self.sum_fresh[:rows, :] = sums[:, :128]
        self.mass_fresh[...] = sums[:, 128:]
        self.top_fresh[...] = jnp.broadcast_to(highest * scale, (rows, 128))

        for copy in self.cache_copies(turn):
            copy.wait()

        @pl.when(turn + 1 < CHUNKS)
        def _():
            for copy in self.cache_copies(turn + 1):
                copy.start()

        self.query_message(turn).wait_recv()

        def beams_step(group, stat):
            for member in range(UNROLL):
                local = group * UNROLL + member
                at = pl.multiple_of(local * 40, 8)
                block = jnp.concatenate(
                    [
                        self.query_rows[turn, pl.ds(at, 40), :],
                        self.query_in[turn, local].astype(jnp.float32),
                    ],
                    0,
                ).astype(jnp.bfloat16)
                scores = dot_nt(block, self.key_slots[slot, local])
                scores = jnp.where(spot < self.lens[chunk * per + local], scores, masked_score)
                highest = jnp.max(scores, 1, keepdims=True)
                weights = jnp.exp2((scores - highest) * scale).astype(jnp.bfloat16)
                value = self.value_slots[slot, local]
                sums = jnp.dot(
                    weights, jnp.concatenate([value, jnp.ones_like(value)], 1),
                    preferred_element_type=jnp.float32,
                )
                top = jnp.broadcast_to(highest * scale, (80, 128))
                self.part_out[turn, local] = (sums[40:, :128] / sums[40:, 128:]).astype(jnp.bfloat16)
                stat = jnp.where(lane == local, top[40:] + jnp.log2(sums[40:, 128:]), stat)
                near = self.top_fresh[pl.ds(at, 40), :]
                summit = jnp.maximum(top[:40], near)
                here = jnp.exp2(top[:40] - summit)
                there = jnp.exp2(near - summit)
                self.sum_own[turn, pl.ds(at, 40), :] = (
                    sums[:40, :128] * here + self.sum_fresh[pl.ds(at, 40), :] * there
                )
                self.mass_own[turn, pl.ds(at, 40), :] = (
                    sums[:40, 128:] * here + self.mass_fresh[pl.ds(at, 40), :] * there
                )
                self.top_own[turn, pl.ds(at, 40), :] = summit
            return stat

        self.stat_out[turn] = lax.fori_loop(0, per // UNROLL, beams_step, jnp.zeros((40, 128), jnp.float32))
        self.part_message(turn).start()
        self.stat_message(turn).start()

    def combine(self, turn):
        self.part_message(turn).wait_recv()
        self.stat_message(turn).wait_recv()
        lane = lax.broadcasted_iota(jnp.int32, (40, 128), 1)

        def beams_step(group, inner):
            stat = self.stat_in[turn]
            for member in range(UNROLL):
                local = group * UNROLL + member
                at = pl.multiple_of(local * 40, 8)
                other = jnp.sum(jnp.where(lane == local, stat, 0.0), 1, keepdims=True)
                top = self.top_own[turn, pl.ds(at, 40), :]
                summit = jnp.maximum(top, other)
                here = jnp.exp2(top - summit)
                there = jnp.exp2(other - summit)
                total = (
                    self.sum_own[turn, pl.ds(at, 40), :] * here + self.part_in[turn, local].astype(jnp.float32) * there
                )
                mass = self.mass_own[turn, pl.ds(at, 40), :] * here + there
                self.sum_fresh[pl.ds(at, 40), :] = total / mass
            return inner

        lax.fori_loop(0, self.per // UNROLL, beams_step, 0)
        return self.sum_fresh

    def settle(self):
        self.fresh_message().wait_send()

        def one(turn, carry):
            self.query_message(turn).wait_send()
            self.part_message(turn).wait_send()
            self.stat_message(turn).wait_send()
            return carry

        lax.fori_loop(0, CHUNKS, one, 0)


def attention_scratch(beams, span):
    per = beams // CHUNKS
    bf16, f32 = jnp.bfloat16, jnp.float32
    dma = pltpu.SemaphoreType.DMA
    return [
        pltpu.VMEM((CHUNKS, per * 40 + 8, 128), f32),
        pltpu.VMEM((CHUNKS, per, 40, 128), bf16),
        pltpu.VMEM((CHUNKS, per, 40, 128), bf16),
        pltpu.VMEM((beams * 5, 128), bf16),
        pltpu.VMEM((2, per, span, 128), bf16),
        pltpu.VMEM((2, per, span, 128), bf16),
        pltpu.VMEM((CHUNKS, per * 40, 128), f32),
        pltpu.VMEM((CHUNKS, per * 40, 128), f32),
        pltpu.VMEM((CHUNKS, per * 40, 128), f32),
        pltpu.VMEM((per * 40 + 8, 128), f32),
        pltpu.VMEM((per * 40, 128), f32),
        pltpu.VMEM((per * 40, 128), f32),
        pltpu.VMEM((CHUNKS, per, 40, 128), bf16),
        pltpu.VMEM((CHUNKS, per, 40, 128), bf16),
        pltpu.VMEM((CHUNKS, 40, 128), f32),
        pltpu.VMEM((CHUNKS, 40, 128), f32),
        dma((2, 2)), dma((2,)), dma((CHUNKS,)), dma((CHUNKS,)), dma((CHUNKS,)), dma((CHUNKS,)), dma((CHUNKS,)), dma((CHUNKS,)),
    ]


def row_keys(accepted, dest):
    beams = dest.shape[1]
    target = (dest // beams).astype(jnp.float32)
    landing = (dest % beams).astype(jnp.float32)
    over = lax.broadcasted_iota(jnp.int32, (beams, beams), 0)
    lane = lax.broadcasted_iota(jnp.int32, (beams, beams), 1)
    wide = jnp.broadcast_to(target, (beams, beams))
    tall = jnp.sum(jnp.where(over == lane, wide, 0.0), 1, keepdims=True)
    earlier = jnp.logical_and(tall == wide, over < lane)
    position = jnp.sum(jnp.where(earlier, 1.0, 0.0), 0, keepdims=True)
    place = target * (beams // 8) + position
    numbers = jnp.concatenate(
        [place, accepted.astype(jnp.float32), landing, jnp.zeros((5, beams), jnp.float32)], 0
    )
    spread = lax.broadcasted_iota(jnp.int32, (beams, beams * 5), 1) // 5 == lax.broadcasted_iota(
        jnp.int32, (beams, beams * 5), 0
    )
    rows = jnp.dot(
        numbers.astype(jnp.bfloat16), spread.astype(jnp.bfloat16), preferred_element_type=jnp.float32
    )
    return rows[0:1], rows[1:2], rows[2:3]


def step_kernel(
    lens, queries, keys, values, weight, fresh, accepted, dest, mixed, next_kv,
    gathered, weight_here, held_0, held_1, held_2, held_3, inbox_0, inbox_1, inbox_2, inbox_3, parcels, arrived,
    local_sem, far_send, gather_recv, tree_send, tree_recv, parcel_send, parcel_recv, *attention_refs,
):
    row, mp = lax.axis_index("row"), lax.axis_index("mp")
    x, core = row // 2, row % 2
    sibling = {"row": x * 2 + 1 - core, "mp": mp}
    right = {"row": ((x + 1) % 4) * 2 + core, "mp": mp}
    left = {"row": ((x + 3) % 4) * 2 + core, "mp": mp}
    pair = {"row": row, "mp": along(mp, 2)}
    held = (held_0, held_1, held_2, held_3)
    inbox = (inbox_0, inbox_1, inbox_2, inbox_3)
    work = Attention(lens, queries, fresh, keys, values, mp % 2, pair, attention_refs)
    for copy in work.cache_copies(0):
        copy.start()
    weight_copy = pltpu.make_async_copy(weight, weight_here, local_sem.at[0])
    weight_copy.start()

    barrier = pltpu.get_barrier_semaphore()
    for step in range(1, 8):
        pl.semaphore_signal(
            barrier, inc=1, device_id={"row": (row + step) % 8, "mp": mp}, device_id_type=MESH
        )
    for direction in range(4):
        pl.semaphore_signal(
            barrier, inc=1, device_id={"row": row, "mp": along(mp, direction)}, device_id_type=MESH
        )
    pl.semaphore_wait(barrier, 11)

    def send_first(turn, carry):
        work.send_query(turn)

        @pl.when(turn == 0)
        def _():
            work.fresh_message().start()

        return carry

    lax.fori_loop(0, 2, send_first, 0)

    tokens = gathered.shape[2]
    half = gathered.shape[3] // 2

    def gather_message(kind, turn):
        source, target, device = {
            "to_right": (0, 3, right), "to_left": (0, 2, left), "to_sibling": (0, 1, sibling),
            "share_right": (2, 4, sibling), "share_left": (3, 5, sibling), "share_far": (6, 7, sibling),
            "pass_left": (2, 6, left), "pass_right": (3, 6, right),
        }[kind]
        number = GATHER_KINDS.index(kind)
        send, recv = far_send.at[number, turn], gather_recv.at[number, turn]
        if kind in ("pass_left", "pass_right"):
            part = pl.ds(0 if kind == "pass_left" else half, half)
            return remote(
                gathered.at[source, turn, :, part], gathered.at[target, turn, :, part], send, recv, device
            )
        return remote(gathered.at[source, turn], gathered.at[target, turn], send, recv, device)

    def publish(turn, rows):
        for head in range(8):
            gathered[0, turn, :, head * 128 : (head + 1) * 128] = rows[pl.ds(head, tokens, stride=8), :].astype(
                jnp.bfloat16
            )
        for kind in ("to_right", "to_left", "to_sibling"):
            gather_message(kind, turn).start()

    def near(turn):
        gather_message("to_left", turn).wait_recv()
        gather_message("pass_left", turn).start()
        gather_message("share_right", turn).start()
        gather_message("to_right", turn).wait_recv()
        gather_message("pass_right", turn).start()
        gather_message("share_left", turn).start()

    def far(turn):
        gather_message("pass_left", turn).wait_recv()
        gather_message("pass_right", turn).wait_recv()
        gather_message("share_far", turn).start()

    place_row, kept_row, landing_row = row_keys(accepted[...], dest[...])
    place = lax.broadcasted_iota(jnp.int32, (64, 320), 0).astype(jnp.float32)
    draft_of = (lax.broadcasted_iota(jnp.int32, (1, 320), 1) % 5).astype(jnp.float32)
    fresh_rows = fresh[...]
    columns = []
    for draft in range(5):
        taken = jnp.where(jnp.logical_and(draft_of == draft, kept_row > draft), place_row, -1.0)
        columns.append(
            jnp.dot(
                (taken == place).astype(jnp.bfloat16), fresh_rows, preferred_element_type=jnp.float32
            ).astype(jnp.bfloat16)
        )
    first = jnp.where(draft_of == 0, place_row, -1.0)
    label = jnp.sum(jnp.where(first == place, landing_row, 0.0), 1, keepdims=True)
    columns.append(jnp.broadcast_to(label, (64, 128)).astype(jnp.bfloat16))
    for block in range(8):
        for part, column in enumerate(columns):
            parcels[block, :, pl.ds(part * 128, 128)] = column[block * 8 : block * 8 + 8]
    own_parcel = pltpu.make_async_copy(parcels.at[row], arrived.at[row], local_sem.at[1])
    own_parcel.start()
    for step in range(1, 8):
        target = (row + step) % 8
        remote(
            parcels.at[target], arrived.at[row], parcel_send.at[step], parcel_recv.at[row],
            {"row": target, "mp": mp},
        ).start()
    work.fresh_message().wait_recv()
    weight_copy.wait()

    my_bits = bits_of(mp)
    y, z = mp // 4, mp % 4
    over_y = (y, along(mp, 0) // 4, along(mp, 1) // 4, (y + 2) % 4)
    over_z = (z, along(mp, 2) % 4, along(mp, 3) % 4, (z + 2) % 4)
    partners = [along(mp, direction) for direction in range(4)]

    def tree_message(tree, step, phase, block, rest):
        index = phase * 15 + STEP_BASE[step] + rest
        return remote(
            held[tree].at[phase * 16 + block], inbox[tree].at[index], tree_send.at[tree, index],
            tree_recv.at[tree, index], {"row": row, "mp": partners[TREES[tree][step]]},
        ), index

    def first_block(slot):
        shift = jnp.where(slot < 2, 0, jnp.where(slot >= 6, 2, jnp.where(slot % 2 == 0, 1, 3)))
        other = jnp.where(slot < 6, jnp.where(slot < 2, slot, jnp.where(slot >= 4, 1, 0)), slot - 6)
        owner = ((x + shift) % 4) * 2 + jnp.where(other == 1, 1 - core, core)
        return owner * 2

    def block_of(couple, piece):
        return first_block(couple * 2 + piece // 2) + piece % 2

    def product_unit(unit):
        phase, couple = unit // 4, unit % 4
        early = phase * 2

        @pl.when(couple == 0)
        def _():
            for turn in (early, early + 1):
                gather_message("to_sibling", turn).wait_recv()

        @pl.when(couple == 2)
        def _():
            for turn in (early, early + 1):
                gather_message("share_right", turn).wait_recv()
                gather_message("share_left", turn).wait_recv()

        @pl.when(couple == 3)
        def _():
            for turn in (early, early + 1):
                gather_message("share_far", turn).wait_recv()

        operand = gathered[pl.ds(couple * 2, 2), pl.ds(early, 2)].reshape(4 * tokens, gathered.shape[3])
        blocks = [block_of(couple, piece) for piece in range(4)]
        across = [[(a + b) % 2 for a, b in zip(bits_of(block), my_bits)] for block in blocks]
        for tree in range(4):
            product = jnp.dot(
                operand, weight_here[:, STARTS[tree] : STARTS[tree] + WIDTHS[tree]],
                preferred_element_type=jnp.float32,
            ).astype(jnp.bfloat16)
            order = TREES[tree]
            for piece in range(4):
                block, apart = blocks[piece], across[piece]
                held[tree][phase * 16 + block] = product[piece * tokens : (piece + 1) * tokens]

                @pl.when(apart[order[0]] == 1)
                def _(tree=tree, block=block, apart=apart, order=order):
                    rest = apart[order[1]] + 2 * apart[order[2]] + 4 * apart[order[3]]
                    tree_message(tree, 0, phase, block, rest)[0].start()

    def receive_step(step, phase):
        count = 1 << (3 - step)
        for rest in sorted(range(count), key=lambda number: (1 - number % 2, number)):
            for tree in range(4):
                apart = [0, 0, 0, 0]
                for later in range(step + 1, 4):
                    apart[TREES[tree][later]] = (rest >> (later - step - 1)) & 1
                block = over_y[apart[0] + 2 * apart[1]] * 4 + over_z[apart[2] + 2 * apart[3]]
                message, index = tree_message(tree, step, phase, block, rest)
                message.wait_recv()
                at = phase * 16 + block
                total = held[tree][at].astype(jnp.float32) + inbox[tree][index].astype(jnp.float32)
                if step == 3:
                    out = pl.ds(pl.multiple_of(phase * tokens, 16), tokens)
                    mixed[out, STARTS[tree] : STARTS[tree] + WIDTHS[tree]] = total.astype(jnp.bfloat16)
                else:
                    held[tree][at] = total.astype(jnp.bfloat16)
                    if rest % 2 == 1:
                        tree_message(tree, step + 1, phase, block, rest // 2)[0].start()

    actions = {
        "S": work.send_query,
        "C": work.attend,
        "K": lambda turn: publish(turn, work.combine(turn)),
        "N": near,
        "F": far,
        "D": product_unit,
    }

    def tick(time, carry):
        for kind, action in actions.items():
            spots = [(spot, int(name[1])) for spot, name in enumerate(WORK) if name[0] == kind]

            @pl.when(any_of([time == spot for spot, _ in spots]))
            def _(action=action, spots=spots):
                action(sum(jnp.where(time == spot, number, 0) for spot, number in spots))

        for step in range(4):
            early, late = WORK.index(f"A{step}"), WORK.index(f"B{step}")

            @pl.when(jnp.logical_or(time == early, time == late))
            def _(step=step, late=late):
                receive_step(step, jnp.where(time == late, 1, 0))

        return carry

    lax.fori_loop(0, len(WORK), tick, 0)

    own_parcel.wait()
    for step in range(1, 8):
        source = (row + 8 - step) % 8
        remote(
            parcels.at[source], arrived.at[source], parcel_send.at[step], parcel_recv.at[source],
            {"row": source, "mp": mp},
        ).wait_recv()
    rows = jnp.concatenate([arrived[block] for block in range(8)], 0)
    slots = lax.broadcasted_iota(jnp.int32, (64, 64), 1).astype(jnp.float32)
    placer = (rows[:, 640:704].astype(jnp.float32) == slots).astype(jnp.bfloat16)
    placed = lax.dot_general(
        placer, rows[:, :640], (((0,), (0,)), ((), ())), preferred_element_type=jnp.float32
    ).astype(jnp.bfloat16)
    for draft in range(5):
        next_kv[draft] = placed[:, draft * 128 : (draft + 1) * 128]

    def settle_gather(turn, carry):
        for kind in GATHER_KINDS:
            gather_message(kind, turn).wait_send()
        return carry

    lax.fori_loop(0, CHUNKS, settle_gather, 0)
    work.settle()
    for step in range(1, 8):
        target = (row + step) % 8
        remote(
            parcels.at[target], arrived.at[row], parcel_send.at[step], parcel_recv.at[row],
            {"row": target, "mp": mp},
        ).wait_send()

    def settle(index, carry):
        for tree in range(4):
            remote(
                held[tree].at[0], inbox[tree].at[index], tree_send.at[tree, index], tree_recv.at[tree, index],
                {"row": row, "mp": partners[0]},
            ).wait_send()
        return carry

    lax.fori_loop(0, 30, settle, 0)


def step(lens, queries, keys, values, weight, fresh, accepted, dest):
    tokens, depth = queries.shape
    columns = weight.shape[1]
    beams, span = keys.shape[0], keys.shape[1]
    rows_owned = tokens // 2
    piece = tokens // CHUNKS
    bf16 = jnp.bfloat16
    dma = pltpu.SemaphoreType.DMA
    vmem = pl.BlockSpec(memory_space=pltpu.VMEM)
    hbm = pl.BlockSpec(memory_space=pl.ANY)
    return pl.pallas_call(
        step_kernel,
        out_shape=(
            jax.ShapeDtypeStruct((rows_owned, columns), bf16),
            jax.ShapeDtypeStruct((5, beams, 128), bf16),
        ),
        in_specs=[pl.BlockSpec(memory_space=pltpu.SMEM), vmem, hbm, hbm, hbm, vmem, vmem, vmem],
        out_specs=(vmem, vmem),
        scratch_shapes=[
            pltpu.VMEM((8, CHUNKS, piece, depth), bf16),
            pltpu.VMEM((depth, columns), bf16),
            *[pltpu.VMEM((32, piece, width), bf16) for width in WIDTHS],
            *[pltpu.VMEM((30, piece, width), bf16) for width in WIDTHS],
            pltpu.VMEM((8, 8, 768), bf16),
            pltpu.VMEM((8, 8, 768), bf16),
            dma((2,)), dma((8, CHUNKS)), dma((8, CHUNKS)), dma((4, 30)), dma((4, 30)), dma((8,)), dma((8,)),
            *attention_scratch(beams, span),
        ],
        compiler_params=pltpu.CompilerParams(
            collective_id=0, has_side_effects=True, vmem_limit_bytes=60 * 1024 * 1024
        ),
        name="step",
    )(lens, queries, keys, values, weight, fresh, accepted, dest)


def hand_on_kernel(mixed, moved, mixed_out, moved_out):
    mixed_out[...] = mixed[...]
    moved_out[...] = moved[...]


def hand_on(mixed, moved):
    vmem = pl.BlockSpec(memory_space=pltpu.VMEM)
    return pl.pallas_call(
        hand_on_kernel,
        out_shape=(
            jax.ShapeDtypeStruct(mixed.shape, mixed.dtype),
            jax.ShapeDtypeStruct(moved.shape, moved.dtype),
        ),
        in_specs=[vmem, vmem],
        out_specs=(vmem, vmem),
        name="hand_on",
    )(mixed, moved)


def shards(queries, new_kv, cache_keys, cache_values, cache_lens, accepted, dest, out_weight):
    beams, _, span, size = cache_keys.shape
    mixed, moved = step(
        cache_lens, queries, cache_keys.reshape(beams, span, size), cache_values.reshape(beams, span, size),
        out_weight, new_kv, accepted.reshape(1, beams), dest.reshape(1, beams),
    )
    mixed, moved = hand_on(mixed, moved)
    return mixed, moved.transpose(1, 0, 2)


def solution(mesh):
    placed = (
        P("row", "mp"),
        P("row", "mp"),
        P("row", "mp", None, None),
        P("row", "mp", None, None),
        P("row"),
        P("row"),
        P("row"),
        P("mp", "row"),
    )
    return jax.shard_map(
        shards,
        mesh=mesh,
        in_specs=placed,
        out_specs=(P("mp", "row"), P("row", None, "mp")),
        check_vma=False,
    )
```
